128 devices in a mesh: visit: 8 (over x, core), fp: 16 (over y, z).
Axes of the slice: x: 4, y: 4, z: 4, core: 2. Of those that a mesh axis runs over, the one named last changes fastest.
Arguments:
- image: bfloat16 [8, 4096, 4096], P('visit', 'fp'), may hold values from -6 to 6
- inv_var: bfloat16 [8, 4096, 4096], P('visit', 'fp'), may hold values from 0.25 to 4
- bg_grid: float32 [8, 16, 16, 128], P('visit', 'fp'), may hold values from -6 to 6
- bg_mix: float32 [16, 16], replicated, may hold values from -1.5 to 1.5
- psf_taps: float32 [8, 16, 21], P('visit', 'fp'), may hold values from 0.05 to 1
- warp_shift: int32 [8, 16], P('visit', 'fp'), may hold values from 0 to 63
- bad_cols: int32 [16, 32], P('fp'), may hold values from 0 to 4095
- piece_patch: int32 [8, 256, 1], P('visit', 'fp'), may hold values from 0 to 15; in each aligned block of 16 rows (0 to 15, 16 to 31, ..., all dimensions but the last counted through in order) at most 2 rows name the same one
- piece_pos: int32 [8, 256], P('visit', 'fp'), may hold values from 0 to 440
- band_of_visit: int32 [8], replicated, may hold values from 0 to 3, as said below
Outputs:
- flux_sum: float32 [4, 16, 456, 4096], P(None, 'fp', None, 'visit')
- weight_sum: float32 [4, 16, 456, 4096], P(None, 'fp', None, 'visit')
The draws below stay inside these ranges and needn't reach their ends.
Inputs may be any that keep to these rules, and one draw needn't show every extreme that they name: `piece_patch`: among the 16 pieces of one CCD group in one visit, at most 2 name the same patch; some group names a patch exactly 2 times. `band_of_visit`: each band is named by exactly 2 visits.
All inputs are finite; a program needn't handle non-finite values.
Results may differ from the reference program's by a relative error of at most 0.0055.
Values may be sent and summed in bfloat16 or wider, within the bound.
No kernel may reach another device: no remote copies, remote signals or barrier semaphores. Data moves between devices by JAX's collectives and lax.ppermute only.
A program may use at most 192 MiB of HBM per device.

```python
import math
import jax
import jax.numpy as jnp
import numpy as np
from jax import lax

ROW_PIX = 4096
BANDS = 4
CCD_ROWS = 256
PIECES = 16
MOST = 2
BORDER = 100
BIN_ROWS = 16
BINS = 128
TAPS_HALF = 10
BAD_COUNT = 32
PIECE_ROWS = 16
FRAME = 456
GRID_ROWS = 16
BIN_PIX = 32
TAPS = 21
HALF = 16
N_VISIT = 8
N_FP = 16


def draw_band_of_visit(key, part):
    return jax.random.permutation(key, jnp.arange(N_VISIT, dtype=jnp.int32) % BANDS)


def touch_ends(entries, stream_key, least, high):
    index_at = [jax.random.randint(jax.random.fold_in(stream_key, axis), (), 0, length) for axis, length in enumerate(entries.shape)]
    widest = entries.shape.index(max(entries.shape))
    beside = index_at[:widest] + [(index_at[widest] + 1) % entries.shape[widest]] + index_at[widest + 1:]
    return entries.at[tuple(index_at)].set(least).at[tuple(beside)].set(high)


def levels(key, shape, shards, smallest, top_value):
    def one(axis_at, shards_of):
        heights = jax.random.uniform(jax.random.fold_in(jax.random.fold_in(key, 6), axis_at), (shards_of,), jnp.float32, smallest / len(shards), top_value / len(shards))
        return jnp.repeat(jnp.exp(heights), shape[axis_at] // shards_of).reshape((-1,) + (1,) * (len(shape) - axis_at - 1))

    level = one(*shards[0])
    for cut in shards[1:]:
        level = level * one(*cut)
    return level


def assign_block(own_key, own, number, rows, number_of, top, bound, lean):
    ranking = jax.random.permutation(own_key, number_of)
    heavy_load, ordinary = shares(number_of, rows * top, bound, lean, True), shares(number_of, rows * top, bound, lean, False)
    places = jnp.arange(number_of)

    def named(tallies, turn):
        used = int((tallies > 0).sum())
        fixed = max(1, used // 4)
        moved = fixed + (places - fixed + turn * (used - fixed)) % max(1, number_of - fixed)
        return jnp.zeros((number_of,), jnp.int32).at[ranking[jnp.where(places < fixed, places, moved)]].set(jnp.asarray(tallies, jnp.int32))

    tallies = jnp.where(number % 4 == 0, named(heavy_load, number // 4), named(ordinary, number - number // 4 - 1))
    mixed = jax.random.permutation(jax.random.fold_in(own, 3), number_of)
    giver, sink = mixed[0:number_of // 2 * 2:2], mixed[1:number_of // 2 * 2:2]
    slack = jnp.minimum(tallies[giver] - 1, bound - tallies[sink]) // 2
    slack = jnp.where((giver == ranking[0]) | (sink == ranking[0]) | (tallies[sink] == 0), 0, jnp.maximum(slack, 0))
    moved = jax.random.randint(jax.random.fold_in(own, 4), (number_of // 2,), 0, 1 << 20) % (slack + 1)
    tallies = tallies.at[giver].add(-moved).at[sink].add(moved)
    labels = jnp.searchsorted(jnp.cumsum(tallies), jnp.arange(rows * top), side="right").astype(jnp.int32)
    listing = labels.reshape(top, rows).T
    listing = listing[jax.random.permutation(jax.random.fold_in(own, 1), rows)]
    turn = jax.random.randint(jax.random.fold_in(own, 2), (rows, 1), 0, top)
    return jnp.take_along_axis(listing, (jnp.arange(top)[None, :] + turn) % top, axis=1)


def shares(amount, total, most, slope, full):
    loads = [(1 << 20) // math.isqrt(standing ** slope) + 1 for standing in range(1, amount + 1)]
    largest = most if full else min(most, max(-(-total // amount), total * loads[0] // sum(loads)))
    least = 1 if total - largest >= amount - 1 else 0
    given, spare = [largest] + [least] * (amount - 1), total - largest - least * (amount - 1)
    while spare > 0:
        candidates = [i for i in range(1, amount) if given[i] < largest] or [i for i in range(1, amount) if given[i] < most]
        mass, budget = sum([loads[i] for i in candidates]), spare
        for i in candidates:
            more = min(most - given[i], max(1, budget * loads[i] // mass), spare)
            given[i] = given[i] + more
            spare = spare - more
    return np.array(given)


def scatter_about(key, dims, spread, limit, cuts=(), kind=jnp.bfloat16):
    values = spread * jax.random.normal(key, dims, jnp.float32)
    if cuts:
        values = values * levels(key, dims, cuts, -0.22, 0.18)
    return jnp.clip(values, -limit, limit).astype(kind)


def setup_inputs(seed: int = 0) -> dict:
    seeds = jax.random.split(jax.random.key(seed), 11)
    image = scatter_about(seeds[0], (N_VISIT, N_FP * CCD_ROWS, ROW_PIX), 1.0, 6.0, ((0, 8), (1, 16)))
    inv_var = jnp.clip(jnp.exp(math.log(4.0) - 2.7725887 * jax.random.uniform(seeds[1], (N_VISIT, N_FP * CCD_ROWS, ROW_PIX), jnp.float32) ** levels(seeds[1], (N_VISIT, N_FP * CCD_ROWS, ROW_PIX), ((0, 8), (1, 16)), -0.2, 0.2)), 0.25, 4.0).astype(jnp.bfloat16)
    bg_grid = scatter_about(seeds[2], (N_VISIT, N_FP, GRID_ROWS, BINS), 1.0, 6.0, ((0, 8), (1, 16)), jnp.float32)
    bg_mix = scatter_about(seeds[3], (N_FP, N_FP), N_FP ** -0.5, 1.5, (), jnp.float32)
    psf_taps = jnp.clip(0.05 + 0.95 * jax.random.uniform(seeds[4], (N_VISIT, N_FP, TAPS), jnp.float32) ** levels(seeds[4], (N_VISIT, N_FP, TAPS), ((0, 8), (1, 16)), -0.2, 0.2), 0.05, 1.0)
    warp_shift = touch_ends(jax.random.randint(seeds[5], (N_VISIT, N_FP), 0, 64), jax.random.fold_in(seeds[5], 1), 0, 63).astype(jnp.int32)
    bad_cols = touch_ends(jax.random.randint(seeds[6], (N_FP, BAD_COUNT), 0, ROW_PIX), jax.random.fold_in(seeds[6], 1), 0, ROW_PIX - 1).astype(jnp.int32)
    piece_patch_keys = jax.random.split(jax.random.fold_in(seeds[7], 1), N_VISIT * (N_FP * PIECES) // PIECES)
    piece_patch_turns = jax.random.permutation(jax.random.fold_in(seeds[7], 3), N_VISIT * (N_FP * PIECES) // PIECES)
    piece_patch = jax.vmap(lambda own, number: assign_block(jax.random.fold_in(seeds[7], 2), own, number, PIECES, N_FP, 1, MOST, 2))(piece_patch_keys, piece_patch_turns).reshape((N_VISIT, N_FP * PIECES, 1))
    piece_pos = touch_ends(jax.random.randint(seeds[8], (N_VISIT, N_FP * PIECES), 0, FRAME - PIECE_ROWS + 1), jax.random.fold_in(seeds[8], 1), 0, FRAME - PIECE_ROWS).astype(jnp.int32)
    band_of_visit = draw_band_of_visit(jax.random.fold_in(seeds[10], 71), 0)
    return dict(image=image, inv_var=inv_var, bg_grid=bg_grid, bg_mix=bg_mix, psf_taps=psf_taps, warp_shift=warp_shift, bad_cols=bad_cols, piece_patch=piece_patch, piece_pos=piece_pos, band_of_visit=band_of_visit)


def make_kernel(tap_vals, shift):
    tap_vals = tap_vals / jnp.sum(tap_vals)
    offset = shift.astype(jnp.float32) / 16.0
    tap_steps = jnp.arange(-2, 7, dtype=jnp.int32).astype(jnp.float32)
    lag_values = offset - tap_steps
    lanczos = jnp.where(jnp.abs(lag_values) < 3.0, jnp.sinc(lag_values) * jnp.sinc(lag_values / 3.0), 0.0)
    lanczos = lanczos / jnp.sum(lanczos)
    kernel = jnp.zeros((2 * HALF + 1,), jnp.float32)
    for position in range(9):
        tap_start = position - 2 - TAPS_HALF + HALF
        kernel = kernel + lanczos[position] * jnp.pad(tap_vals, (tap_start, 2 * HALF + 1 - tap_start - tap_vals.shape[0]))
    return kernel


def convolve_taps(pixel_rows, kernel):
    padded = jnp.pad(pixel_rows.astype(jnp.float32), ((0, 0), (HALF, HALF)))
    running = jnp.zeros(pixel_rows.shape, jnp.float32)
    for position in range(2 * HALF + 1):
        running = running + kernel[position].astype(jnp.float32) * padded[:, position:position + ROW_PIX]
    return running


def reference(image, inv_var, bg_grid, bg_mix, psf_taps, warp_shift, bad_cols, piece_patch, piece_pos, band_of_visit):
    columns = jnp.arange(ROW_PIX, dtype=jnp.int32)
    good_cols = 1.0 - jnp.any(bad_cols[:, :, None] == columns[None, None, :], axis=1).astype(jnp.float32)
    edge_rows = 2 * BORDER

    def one_visit(totals, inputs):
        pixels, weights, grids, tap_sets, shifts, patches, starts, band_id = inputs
        bg_model = jnp.einsum('ck,kab->cab', bg_mix, grids, precision=lax.Precision.HIGHEST)
        backdrop = jnp.broadcast_to(bg_model[:, :, None, :, None], (N_FP, GRID_ROWS, BIN_ROWS, BINS, BIN_PIX)).reshape(N_FP, CCD_ROWS, ROW_PIX)
        pixels = pixels.reshape(N_FP, CCD_ROWS, ROW_PIX)
        weights = weights.reshape(N_FP, CCD_ROWS, ROW_PIX)
        flux_in = ((pixels.astype(jnp.float32) - backdrop) * good_cols[:, None, :]).astype(jnp.bfloat16)
        ivar_in = (weights.astype(jnp.float32) * good_cols[:, None, :]).astype(jnp.bfloat16)

        def warp_item(item):
            flux_rows, ivar_rows, tap_row, shift = item
            kernel = make_kernel(tap_row, shift)
            warped_flux = convolve_taps(flux_rows, kernel.astype(jnp.bfloat16)).astype(jnp.bfloat16)
            warped_weight = convolve_taps(ivar_rows, jnp.abs(kernel).astype(jnp.bfloat16)).astype(jnp.bfloat16)
            return warped_flux, warped_weight

        warped_flux, warped_weight = lax.map(warp_item, (flux_in, ivar_in, tap_sets, shifts))
        flux_pieces = warped_flux.reshape(N_FP * PIECES, PIECE_ROWS, ROW_PIX).astype(jnp.float32)
        weight_pieces = warped_weight.reshape(N_FP * PIECES, PIECE_ROWS, ROW_PIX).astype(jnp.float32)
        dest_rows = starts[:, None] + jnp.arange(PIECE_ROWS, dtype=jnp.int32)[None, :]
        targets = jnp.broadcast_to(patches[:, None], dest_rows.shape)
        accum = jnp.zeros((2, N_FP, FRAME, ROW_PIX), jnp.float32)
        accum = accum.at[0, targets, dest_rows].add(weight_pieces * flux_pieces)
        accum = accum.at[1, targets, dest_rows].add(weight_pieces)
        rounded = lax.optimization_barrier(accum.astype(jnp.bfloat16)).astype(jnp.float32)
        empty = jnp.zeros((2, 1, edge_rows, ROW_PIX), jnp.float32)
        from_left = jnp.concatenate([empty, rounded[:, :-1, FRAME - edge_rows:]], axis=1)
        from_right = jnp.concatenate([rounded[:, 1:, :edge_rows], empty], axis=1)
        combined = rounded.at[:, :, :edge_rows].add(from_left)
        combined = combined.at[:, :, FRAME - edge_rows:].add(from_right)
        totals = totals.at[band_id].add(combined)
        return totals, None

    totals = jnp.zeros((BANDS, 2, N_FP, FRAME, ROW_PIX), jnp.float32)
    totals, unused = lax.scan(one_visit, totals, (image, inv_var, bg_grid, psf_taps, warp_shift, piece_patch[:, :, 0], piece_pos, band_of_visit))
    return totals[:, 0], totals[:, 1]
```

```python
import jax
import jax.numpy as jnp
from jax import lax
from jax.experimental import pallas as pl
from jax.experimental.pallas import tpu as pltpu
from jax.sharding import PartitionSpec as P

ROW_PIX = 4096
BANDS = 4
CCD_ROWS = 256
MOST = 2
BORDER = 100
EDGE = 2 * BORDER
TAPS_HALF = 10
FRAME = 456
HALF = 16
TAPS = 2 * HALF + 1
PIECES = 16
PIECE_ROWS = 16
BINS = 128
BIN_PIX = ROW_PIX // BINS
PATCHES = 16
VISITS = 8
SPAN = ROW_PIX // VISITS
BLOCK = 256
PAD = 128
WINDOW = BLOCK + 2 * PAD
UNUSED = 1 << 20
VMEM_LIMIT = 48 << 20


def make_kernel(tap_vals, shift):
    tap_vals = tap_vals / jnp.sum(tap_vals)
    offset = shift.astype(jnp.float32) / 16.0
    tap_steps = jnp.arange(-2, 7, dtype=jnp.int32).astype(jnp.float32)
    lag_values = offset - tap_steps
    lanczos = jnp.where(
        jnp.abs(lag_values) < 3.0, jnp.sinc(lag_values) * jnp.sinc(lag_values / 3.0), 0.0
    )
    lanczos = lanczos / jnp.sum(lanczos)
    kernel = jnp.zeros((TAPS,), jnp.float32)
    for position in range(9):
        tap_start = position - 2 - TAPS_HALF + HALF
        kernel = kernel + lanczos[position] * jnp.pad(
            tap_vals, (tap_start, TAPS - tap_start - tap_vals.shape[0])
        )
    return kernel


def fill_band(taps_ref, band_ref, absolute):
    lag = lax.broadcasted_iota(jnp.int32, (128, 128), 0) - lax.broadcasted_iota(
        jnp.int32, (128, 128), 1
    )
    zero = jnp.zeros((128, 128), jnp.bfloat16)
    tiles = []
    for k in (-1, 0, 1):
        tile = jnp.zeros((128, 128), jnp.float32)
        for d in range(-HALF, HALF + 1):
            want = d - 128 * k
            if -128 < want < 128:
                value = taps_ref[d + HALF]
                value = jnp.abs(value) if absolute else value
                tile = jnp.where(lag == want, value, tile)
        tiles.append(tile.astype(jnp.bfloat16))
    for i in range(WINDOW // 128):
        for o in range(BLOCK // 128):
            k = i - o - 1
            band_ref[128 * i : 128 * (i + 1), 128 * o : 128 * (o + 1)] = (
                tiles[k + 1] if -1 <= k <= 1 else zero
            )


def good_columns(bad_ref):
    columns = lax.broadcasted_iota(jnp.int32, (1, ROW_PIX), 1)
    hit = bad_ref[...] == columns
    return 1.0 - jnp.max(hit.astype(jnp.float32), axis=0, keepdims=True)


def fill_padded(padded_ref, rows, values):
    padded_ref[rows, 0:PAD] = jnp.zeros((values.shape[0], PAD), jnp.bfloat16)
    padded_ref[rows, PAD : PAD + ROW_PIX] = values
    padded_ref[rows, PAD + ROW_PIX :] = jnp.zeros((values.shape[0], PAD), jnp.bfloat16)


def convolve_span(padded_ref, band_ref, span):
    start = pl.multiple_of(span * SPAN, 128)
    parts = [
        jnp.dot(
            padded_ref[:, pl.ds(pl.multiple_of(start + BLOCK * n, 128), WINDOW)],
            band_ref[...],
            preferred_element_type=jnp.float32,
        )
        for n in range(SPAN // BLOCK)
    ]
    return jnp.concatenate(parts, axis=1)


def send_pieces(patch_ref, out_ref, values):
    out_ref[...] = jnp.zeros(out_ref.shape, out_ref.dtype)
    patches = [patch_ref[j] for j in range(PIECES)]
    for j in range(PIECES):
        rank = jnp.int32(0)
        for k in range(j):
            rank = rank + (patches[k] == patches[j]).astype(jnp.int32)
        slot = patches[j] * MOST + jnp.minimum(rank, MOST - 1)
        out_ref[0, slot] = values[PIECE_ROWS * j : PIECE_ROWS * (j + 1)]


def weight_body(taps_ref, patch_ref, ivar_ref, bad_ref, send_ref, weight_ref, padded_ref, band_ref):
    span = pl.program_id(0)

    @pl.when(span == 0)
    def _():
        good = good_columns(bad_ref).astype(jnp.bfloat16)
        fill_padded(padded_ref, slice(0, CCD_ROWS), ivar_ref[...] * good)
        fill_band(taps_ref, band_ref, True)

    weight = convolve_span(padded_ref, band_ref, span).astype(jnp.bfloat16)
    weight_ref[...] = weight
    send_pieces(patch_ref, send_ref, weight)


def flux_body(
    taps_ref, patch_ref, mix_ref, image_ref, bad_ref, grids_ref, weight_ref, send_ref, padded_ref, band_ref
):
    span = pl.program_id(0)

    @pl.when(span == 0)
    def _():
        good = good_columns(bad_ref)
        fill_padded(padded_ref, slice(0, CCD_ROWS), image_ref[...] * good.astype(jnp.bfloat16))
        model = mix_ref[0] * grids_ref[0]
        for k in range(1, PIECES):
            model = model + mix_ref[k] * grids_ref[k]
        upper = model.astype(jnp.bfloat16)
        lower = (model - upper.astype(jnp.float32)).astype(jnp.bfloat16)
        both = jnp.concatenate([upper, lower], axis=0)
        spread = (
            lax.broadcasted_iota(jnp.int32, (BINS, ROW_PIX), 1) // BIN_PIX
            == lax.broadcasted_iota(jnp.int32, (BINS, ROW_PIX), 0)
        ).astype(jnp.bfloat16)
        expanded = jnp.dot(both, spread, preferred_element_type=jnp.float32) * good
        fill_padded(
            padded_ref, slice(CCD_ROWS, CCD_ROWS + 2 * PIECES), expanded.astype(jnp.bfloat16)
        )
        fill_band(taps_ref, band_ref, False)

    warped = convolve_span(padded_ref, band_ref, span)
    backdrop = (
        warped[CCD_ROWS : CCD_ROWS + PIECES] + warped[CCD_ROWS + PIECES : CCD_ROWS + 2 * PIECES]
    )
    backdrop = jnp.broadcast_to(backdrop[:, None, :], (PIECES, PIECE_ROWS, SPAN)).reshape(
        CCD_ROWS, SPAN
    )
    flux = warped[:CCD_ROWS] - backdrop
    send_pieces(
        patch_ref, send_ref, (flux * weight_ref[...].astype(jnp.float32)).astype(jnp.bfloat16)
    )


def scatter_body(band_ref, rows_ref, received_ref, total_ref, low_ref, high_ref):
    visit = pl.program_id(0)

    @pl.when(visit == 0)
    def _():
        total_ref[...] = jnp.zeros(total_ref.shape, total_ref.dtype)

    slots = rows_ref.shape[-1]
    place = lax.broadcasted_iota(jnp.int32, (FRAME, slots), 0) == rows_ref[0]
    frames = jnp.dot(
        place.astype(jnp.bfloat16), received_ref[0], preferred_element_type=jnp.float32
    )
    band = band_ref[visit]
    total_ref[band] = total_ref[band] + frames

    @pl.when(visit == pl.num_programs(0) - 1)
    def _():
        low_ref[...] = total_ref[:, :EDGE].astype(jnp.bfloat16)
        high_ref[...] = total_ref[:, FRAME - EDGE :].astype(jnp.bfloat16)


def merge_body(total_ref, before_ref, after_ref, out_ref):
    total = total_ref[0]
    out_ref[0, :EDGE] = total[:EDGE] + before_ref[0].astype(jnp.float32)
    out_ref[0, EDGE : FRAME - EDGE] = total[EDGE : FRAME - EDGE]
    out_ref[0, FRAME - EDGE :] = total[FRAME - EDGE :] + after_ref[0].astype(jnp.float32)


SMEM = pl.BlockSpec(memory_space=pltpu.SMEM)


def whole(shape):
    zeros = (0,) * len(shape)
    return pl.BlockSpec(shape, lambda i: zeros)


PARAMS = pltpu.CompilerParams(
    dimension_semantics=("arbitrary",), vmem_limit_bytes=VMEM_LIMIT
)
SEND_SHAPE = (VISITS, PATCHES * MOST, PIECE_ROWS, SPAN)
SEND_BLOCK = pl.BlockSpec((1, PATCHES * MOST, PIECE_ROWS, SPAN), lambda i: (i, 0, 0, 0))
SPAN_BLOCK = pl.BlockSpec((CCD_ROWS, SPAN), lambda i: (0, i))


def send_weight(taps, patches, inv_var, bad):
    return pl.pallas_call(
        weight_body,
        grid=(VISITS,),
        in_specs=[SMEM, SMEM, whole(inv_var.shape), whole(bad.shape)],
        out_specs=[SEND_BLOCK, SPAN_BLOCK],
        out_shape=[
            jax.ShapeDtypeStruct(SEND_SHAPE, jnp.bfloat16),
            jax.ShapeDtypeStruct((CCD_ROWS, ROW_PIX), jnp.bfloat16),
        ],
        scratch_shapes=[
            pltpu.VMEM((CCD_ROWS, ROW_PIX + 2 * PAD), jnp.bfloat16),
            pltpu.VMEM((WINDOW, BLOCK), jnp.bfloat16),
        ],
        compiler_params=PARAMS,
        name="send_weight",
    )(taps, patches, inv_var, bad)


def send_flux(taps, patches, mix_row, image, bad, grids, weight):
    return pl.pallas_call(
        flux_body,
        grid=(VISITS,),
        in_specs=[
            SMEM,
            SMEM,
            SMEM,
            whole(image.shape),
            whole(bad.shape),
            whole(grids.shape),
            SPAN_BLOCK,
        ],
        out_specs=SEND_BLOCK,
        out_shape=jax.ShapeDtypeStruct(SEND_SHAPE, jnp.bfloat16),
        scratch_shapes=[
            pltpu.VMEM((CCD_ROWS + 2 * PIECES, ROW_PIX + 2 * PAD), jnp.bfloat16),
            pltpu.VMEM((WINDOW, BLOCK), jnp.bfloat16),
        ],
        compiler_params=PARAMS,
        name="send_flux",
    )(taps, patches, mix_row, image, bad, grids, weight)


def exchange(pieces):
    sent = pieces.reshape(VISITS * PATCHES, MOST, PIECE_ROWS, SPAN)
    return lax.all_to_all(sent, ("visit", "fp"), split_axis=0, concat_axis=0, tiled=True)


def scatter(band_of_visit, dest_rows, received):
    slots = PATCHES * MOST * PIECE_ROWS
    return pl.pallas_call(
        scatter_body,
        grid=(VISITS,),
        in_specs=[
            SMEM,
            pl.BlockSpec((1, 1, slots), lambda i: (i, 0, 0)),
            pl.BlockSpec((1, slots, SPAN), lambda i: (i, 0, 0)),
        ],
        out_specs=[
            whole((BANDS, FRAME, SPAN)),
            whole((BANDS, EDGE, SPAN)),
            whole((BANDS, EDGE, SPAN)),
        ],
        out_shape=[
            jax.ShapeDtypeStruct((BANDS, FRAME, SPAN), jnp.float32),
            jax.ShapeDtypeStruct((BANDS, EDGE, SPAN), jnp.bfloat16),
            jax.ShapeDtypeStruct((BANDS, EDGE, SPAN), jnp.bfloat16),
        ],
        compiler_params=PARAMS,
        name="scatter",
    )(band_of_visit, dest_rows, received.reshape(VISITS, slots, SPAN))


def merge(total, before, after):
    edge = pl.BlockSpec((1, EDGE, SPAN), lambda i: (i, 0, 0))
    frame = pl.BlockSpec((1, FRAME, SPAN), lambda i: (i, 0, 0))
    return pl.pallas_call(
        merge_body,
        grid=(BANDS,),
        in_specs=[frame, edge, edge],
        out_specs=frame,
        out_shape=jax.ShapeDtypeStruct((BANDS, FRAME, SPAN), jnp.float32),
        compiler_params=PARAMS,
        name="merge",
    )(total, before, after)


def borders(total, low, high):
    peers = lax.axis_size("fp")
    up = [(i, i + 1) for i in range(peers - 1)]
    down = [(j, i) for i, j in up]
    return merge(total, lax.ppermute(high, "fp", up), lax.ppermute(low, "fp", down))


def slot_rows(patches, starts):
    piece_ids = jnp.arange(PIECES, dtype=jnp.int32)
    earlier = piece_ids[:, None] > piece_ids[None, :]
    rank = jnp.sum((earlier & (patches[:, None] == patches[None, :])).astype(jnp.int32), axis=1)
    slot = patches * MOST + rank
    chosen = slot[None, :] == jnp.arange(PATCHES * MOST, dtype=jnp.int32)[:, None]
    start = jnp.sum(jnp.where(chosen, starts[None, :] - UNUSED, 0), axis=1) + UNUSED
    everywhere = jnp.broadcast_to(start.reshape(1, PATCHES, MOST), (VISITS, PATCHES, MOST))
    arrived = lax.all_to_all(
        everywhere.reshape(VISITS * PATCHES, MOST),
        ("visit", "fp"),
        split_axis=0,
        concat_axis=0,
        tiled=True,
    )
    rows = arrived[:, :, None] + jnp.arange(PIECE_ROWS, dtype=jnp.int32)
    return rows.reshape(VISITS, 1, PATCHES * MOST * PIECE_ROWS)


def shards(
    image,
    inv_var,
    bg_grid,
    bg_mix,
    psf_taps,
    warp_shift,
    bad_cols,
    piece_patch,
    piece_pos,
    band_of_visit,
):
    grids = lax.all_gather(bg_grid, "fp", axis=1, tiled=True)[0]
    mix_row = lax.dynamic_slice_in_dim(bg_mix, lax.axis_index("fp"), 1, 0)[0]
    patches = piece_patch[0, :, 0]
    dest_rows = slot_rows(patches, piece_pos[0])
    taps = make_kernel(psf_taps[0, 0], warp_shift[0, 0])
    bad = bad_cols.reshape(-1, 1)
    weight_pieces, weight = send_weight(taps, patches, inv_var[0], bad)
    weight_arrived = exchange(weight_pieces)
    flux_pieces = send_flux(taps, patches, mix_row, image[0], bad, grids, weight)
    flux_arrived = exchange(flux_pieces)
    weight_out = borders(*scatter(band_of_visit, dest_rows, weight_arrived))
    flux_out = borders(*scatter(band_of_visit, dest_rows, flux_arrived))
    return (flux_out[:, None], weight_out[:, None])


def solution(mesh):
    placed = (
        P("visit", "fp", None),
        P("visit", "fp", None),
        P("visit", "fp", None, None),
        P(),
        P("visit", "fp", None),
        P("visit", "fp"),
        P("fp", None),
        P("visit", "fp", None),
        P("visit", "fp"),
        P(),
    )
    return jax.shard_map(
        shards,
        mesh=mesh,
        in_specs=placed,
        out_specs=(P(None, "fp", None, "visit"), P(None, "fp", None, "visit")),
        check_vma=False,
    )
```

```python
import functools

import jax
import jax.numpy as jnp
from jax import lax
from jax.experimental import pallas as pl
from jax.experimental.pallas import tpu as pltpu
from jax.sharding import PartitionSpec as P

ROW_PIX = 4096
BANDS = 4
CCD_ROWS = 256
MOST = 2
BORDER = 100
EDGE = 2 * BORDER
TAPS_HALF = 10
FRAME = 456
HALF = 16
TAPS = 2 * HALF + 1
PIECES = 16
PIECE_ROWS = 16
BINS = 128
BIN_PIX = ROW_PIX // BINS
PATCHES = 16
VISITS = 8
GROUPS = 16
GRID_ROWS = 16
PACKED = GRID_ROWS + 8
SPAN = ROW_PIX // VISITS
CHUNKS = 1
BLOCK = 256
PAD = 128
WINDOW = BLOCK + 2 * PAD
UNUSED = 1 << 20
WIDTH = SPAN // CHUNKS


def fill_band(psf_ref, shift_ref, band_ref, absolute):
    shape = (16, WINDOW)
    step = lax.broadcasted_iota(jnp.int32, shape, 0) - 2
    lag = 3 * PAD - lax.broadcasted_iota(jnp.int32, shape, 1) - step
    offset = (shift_ref[0, 0] - 16 * step).astype(jnp.float32) / 16.0
    angle = offset * jnp.float32(jnp.pi)
    safe = jnp.where(offset == 0.0, 1.0, angle)
    lanczos = jnp.where(
        offset == 0.0, 1.0, 3.0 * jnp.sin(safe) * jnp.sin(safe / 3.0) / (safe * safe)
    )
    lanczos = jnp.where((jnp.abs(offset) < 3.0) & (step < 7), lanczos, 0.0)
    lanczos = lanczos / jnp.sum(lanczos, axis=0, keepdims=True)
    taps = jnp.zeros(shape, jnp.float32)
    total = psf_ref[0, 0, 0]
    for e in range(2 * TAPS_HALF + 1):
        value = psf_ref[0, 0, e]
        taps = jnp.where(lag == e - TAPS_HALF, value, taps)
        total = total + value if e else total
    combined = jnp.sum(lanczos * (taps / total), axis=0, keepdims=True)
    combined = jnp.abs(combined) if absolute else combined
    rolled = pltpu.roll(
        jnp.broadcast_to(combined, (128, WINDOW)), 0, axis=1, stride=1, stride_axis=0
    ).astype(jnp.bfloat16)
    for i in range(WINDOW // 128):
        for o in range(BLOCK // 128):
            tile = (o - i) % (WINDOW // 128)
            band_ref[128 * i : 128 * (i + 1), 128 * o : 128 * (o + 1)] = rolled[
                :, 128 * tile : 128 * (tile + 1)
            ]


def fill_good(bad_ref, good_ref):
    columns = lax.broadcasted_iota(jnp.int32, good_ref.shape, 1) - PAD
    good = (columns >= 0) & (columns < ROW_PIX)
    for k in range(bad_ref.shape[-1]):
        good = good & (columns != bad_ref[0, k])
    good_ref[...] = good.astype(jnp.float32)


def convolve(window, band_ref, width):
    parts = [
        jnp.dot(
            window[:, BLOCK * n : BLOCK * n + WINDOW],
            band_ref[...],
            preferred_element_type=jnp.float32,
        )
        for n in range(width // BLOCK)
    ]
    return parts[0] if len(parts) == 1 else jnp.concatenate(parts, axis=1)


def send_pieces(patch_ref, out_ref, values):
    out_ref[...] = jnp.zeros(out_ref.shape, out_ref.dtype)
    patches = [patch_ref[j] for j in range(PIECES)]
    for j in range(PIECES):
        rank = jnp.int32(0)
        for k in range(j):
            rank = rank + (patches[k] == patches[j]).astype(jnp.int32)
        slot = patches[j] * MOST + jnp.minimum(rank, MOST - 1)
        out_ref[0, slot] = values[PIECE_ROWS * j : PIECE_ROWS * (j + 1)]


def pack_body(where_ref, mix_ref, patch_ref, pos_ref, grid_ref, out_ref):
    group = where_ref[1]
    shape = (PATCHES, BINS)
    patch = lax.broadcasted_iota(jnp.int32, shape, 0)
    slot = lax.broadcasted_iota(jnp.int32, shape, 1)
    first = jnp.full(shape, UNUSED, jnp.int32)
    patches = [patch_ref[j] for j in range(PIECES)]
    for j in range(PIECES):
        rank = jnp.int32(0)
        for k in range(j):
            rank = rank + (patches[k] == patches[j]).astype(jnp.int32)
        first = jnp.where((patch == patches[j]) & (slot == rank), pos_ref[0, j], first)
    first = first.astype(jnp.float32)
    for q in range(PATCHES):
        out_ref[q, :GRID_ROWS] = grid_ref[0, 0] * mix_ref[q, group]
        out_ref[q, GRID_ROWS:] = jnp.broadcast_to(first[q : q + 1], (PACKED - GRID_ROWS, BINS))


def masked_window(chunk, good_ref, left_ref, mid_ref, right_ref):
    width = mid_ref.shape[-1]
    start = pl.multiple_of(pl.program_id(0) * SPAN + chunk * width, 128)
    good = good_ref[:, pl.ds(start, width + 2 * PAD)]
    window = jnp.concatenate([left_ref[0], mid_ref[0], right_ref[0]], axis=1)
    return start, good, window * good.astype(jnp.bfloat16)


def weight_body(
    chunk,
    psf_ref,
    shift_ref,
    patch_ref,
    bad_ref,
    left_ref,
    mid_ref,
    right_ref,
    send_ref,
    weight_ref,
    good_ref,
    band_ref,
):
    @pl.when(pl.program_id(0) == 0)
    def _():
        fill_good(bad_ref, good_ref)
        fill_band(psf_ref, shift_ref, band_ref, True)

    _, _, window = masked_window(chunk, good_ref, left_ref, mid_ref, right_ref)
    weight = convolve(window, band_ref, mid_ref.shape[-1]).astype(jnp.bfloat16)
    weight_ref[0] = weight
    send_pieces(patch_ref, send_ref, weight)


def flux_body(
    chunk,
    psf_ref,
    shift_ref,
    patch_ref,
    bad_ref,
    left_ref,
    mid_ref,
    right_ref,
    packed_ref,
    weight_ref,
    send_ref,
    good_ref,
    band_ref,
    model_ref,
):
    @pl.when(pl.program_id(0) == 0)
    def _():
        fill_good(bad_ref, good_ref)
        fill_band(psf_ref, shift_ref, band_ref, False)
        model = packed_ref[0, :GRID_ROWS]
        for k in range(1, GROUPS):
            model = model + packed_ref[k, :GRID_ROWS]
        upper = model.astype(jnp.bfloat16)
        model_ref[:GRID_ROWS] = upper
        model_ref[GRID_ROWS:] = (model - upper.astype(jnp.float32)).astype(jnp.bfloat16)

    width = mid_ref.shape[-1]
    start, good, window = masked_window(chunk, good_ref, left_ref, mid_ref, right_ref)
    shape = (BINS, width + 2 * PAD)
    first = lax.broadcasted_iota(jnp.int32, shape, 0) * BIN_PIX
    column = lax.broadcasted_iota(jnp.int32, shape, 1) + (start - PAD)
    spread = ((column >= first) & (column < first + BIN_PIX)).astype(jnp.bfloat16)
    expanded = jnp.dot(model_ref[...], spread, preferred_element_type=jnp.float32) * good
    warped = convolve(
        jnp.concatenate([window, expanded.astype(jnp.bfloat16)], axis=0), band_ref, width
    )
    backdrop = warped[CCD_ROWS : CCD_ROWS + GRID_ROWS] + warped[CCD_ROWS + GRID_ROWS :]
    backdrop = jnp.broadcast_to(
        backdrop[:, None, :], (GRID_ROWS, CCD_ROWS // GRID_ROWS, width)
    ).reshape(CCD_ROWS, width)
    flux = warped[:CCD_ROWS] - backdrop
    send_pieces(
        patch_ref, send_ref, (flux * weight_ref[0].astype(jnp.float32)).astype(jnp.bfloat16)
    )


def scatter_body(where_ref, band_ref, rows_ref, received_ref, total_ref, low_ref, high_ref):
    visit = pl.program_id(0)

    @pl.when(visit == 0)
    def _():
        total_ref[...] = jnp.zeros(total_ref.shape, total_ref.dtype)

    slots = rows_ref.shape[-1]
    place = lax.broadcasted_iota(jnp.int32, (FRAME, slots), 0) == rows_ref[0]
    frames = jnp.dot(
        place.astype(jnp.bfloat16), received_ref[0], preferred_element_type=jnp.float32
    )
    band = band_ref[visit]
    total_ref[band] = total_ref[band] + frames

    @pl.when(visit == pl.num_programs(0) - 1)
    def _():
        low_ref[...] = total_ref[:, :EDGE].astype(jnp.bfloat16)
        high_ref[...] = total_ref[:, FRAME - EDGE :].astype(jnp.bfloat16)


def merge_body(total_ref, before_ref, after_ref, *refs):
    out_ref = refs[-1]
    total = total_ref[0]
    out_ref[0, :EDGE] = total[:EDGE] + before_ref[0].astype(jnp.float32)
    out_ref[0, EDGE : FRAME - EDGE] = total[EDGE : FRAME - EDGE]
    out_ref[0, FRAME - EDGE :] = total[FRAME - EDGE :] + after_ref[0].astype(jnp.float32)


SMEM = pl.BlockSpec(memory_space=pltpu.SMEM)


def whole(shape):
    zeros = (0,) * len(shape)
    return pl.BlockSpec(shape, lambda i, *_: zeros)


def params(mebibytes):
    return pltpu.CompilerParams(
        dimension_semantics=("arbitrary",), vmem_limit_bytes=mebibytes << 20
    )


def window_specs(chunk):
    per = SPAN // WIDTH
    tiles = WIDTH // 128
    last = ROW_PIX // 128 - 1
    left = pl.BlockSpec(
        (1, CCD_ROWS, 128),
        lambda i, *_: (0, 0, jnp.maximum((per * i + chunk) * tiles - 1, 0)),
    )
    mid = pl.BlockSpec((1, CCD_ROWS, WIDTH), lambda i, *_: (0, 0, per * i + chunk))
    right = pl.BlockSpec(
        (1, CCD_ROWS, 128),
        lambda i, *_: (0, 0, jnp.minimum((per * i + chunk + 1) * tiles, last)),
    )
    return [left, mid, right]


SEND_SHAPE = (VISITS, PATCHES * MOST, PIECE_ROWS, WIDTH)
SEND_BLOCK = pl.BlockSpec((1,) + SEND_SHAPE[1:], lambda i, *_: (i, 0, 0, 0))
WEIGHT_BLOCK = pl.BlockSpec((1, CCD_ROWS, WIDTH), lambda i, *_: (i, 0, 0))
GOOD_SCRATCH = pltpu.VMEM((1, ROW_PIX + 2 * PAD), jnp.float32)
BAND_SCRATCH = pltpu.VMEM((WINDOW, BLOCK), jnp.bfloat16)


def send_weight(chunk, psf, shift, patches, bad, inv_var):
    return pl.pallas_call(
        functools.partial(weight_body, chunk),
        grid=(VISITS,),
        in_specs=[SMEM] * 4 + window_specs(chunk),
        out_specs=[SEND_BLOCK, WEIGHT_BLOCK],
        out_shape=[
            jax.ShapeDtypeStruct(SEND_SHAPE, jnp.bfloat16),
            jax.ShapeDtypeStruct((VISITS, CCD_ROWS, WIDTH), jnp.bfloat16),
        ],
        scratch_shapes=[GOOD_SCRATCH, BAND_SCRATCH],
        compiler_params=params(48),
        name="send_weight",
    )(psf, shift, patches, bad, inv_var, inv_var, inv_var)


def pack(where, mix, patches, starts, grid):
    return pl.pallas_call(
        pack_body,
        in_specs=[SMEM] * 4 + [pl.BlockSpec(memory_space=pltpu.VMEM)],
        out_specs=pl.BlockSpec(memory_space=pltpu.VMEM),
        out_shape=jax.ShapeDtypeStruct((PATCHES, PACKED, BINS), jnp.float32),
        name="pack",
    )(where, mix, patches, starts, grid)


def send_flux(chunk, psf, shift, patches, bad, image, packed, weight):
    return pl.pallas_call(
        functools.partial(flux_body, chunk),
        grid=(VISITS,),
        in_specs=[SMEM] * 4 + window_specs(chunk) + [whole(packed.shape), WEIGHT_BLOCK],
        out_specs=SEND_BLOCK,
        out_shape=jax.ShapeDtypeStruct(SEND_SHAPE, jnp.bfloat16),
        scratch_shapes=[
            GOOD_SCRATCH,
            BAND_SCRATCH,
            pltpu.VMEM((2 * GRID_ROWS, BINS), jnp.bfloat16),
        ],
        compiler_params=params(48),
        name="send_flux",
    )(psf, shift, patches, bad, image, image, image, packed, weight)


def exchange(pieces):
    sent = pieces.reshape(VISITS * PATCHES, MOST, PIECE_ROWS, WIDTH)
    return lax.all_to_all(sent, ("visit", "fp"), split_axis=0, concat_axis=0, tiled=True)


def scatter(where, band_of_visit, dest_rows, received):
    slots = PATCHES * MOST * PIECE_ROWS
    shapes = [
        jax.ShapeDtypeStruct((BANDS, FRAME, WIDTH), jnp.float32),
        jax.ShapeDtypeStruct((BANDS, EDGE, WIDTH), jnp.bfloat16),
        jax.ShapeDtypeStruct((BANDS, EDGE, WIDTH), jnp.bfloat16),
    ]
    return pl.pallas_call(
        scatter_body,
        grid_spec=pltpu.PrefetchScalarGridSpec(
            num_scalar_prefetch=1,
            grid=(VISITS,),
            in_specs=[
                SMEM,
                pl.BlockSpec((1, 1, slots), lambda i, at: ((at[0] - i) & (VISITS - 1), 0, 0)),
                pl.BlockSpec((1, slots, WIDTH), lambda i, at: (i, 0, 0)),
            ],
            out_specs=[whole(shape.shape) for shape in shapes],
        ),
        out_shape=shapes,
        compiler_params=params(20),
        name="scatter",
    )(where, band_of_visit, dest_rows, received.reshape(VISITS, slots, WIDTH))


def merge(chunk, total, before, after, earlier):
    edge = pl.BlockSpec((1, EDGE, WIDTH), lambda i: (i, 0, 0))
    frame = pl.BlockSpec((1, FRAME, WIDTH), lambda i: (i, 0, 0))
    return pl.pallas_call(
        merge_body,
        grid=(BANDS,),
        in_specs=[frame, edge, edge] + [pl.BlockSpec(memory_space=pl.ANY)] * len(earlier),
        out_specs=pl.BlockSpec((1, FRAME, WIDTH), lambda i: (i, 0, chunk)),
        out_shape=jax.ShapeDtypeStruct((BANDS, FRAME, SPAN), jnp.float32),
        input_output_aliases={3: 0} if earlier else {},
        compiler_params=params(16),
        name="merge",
    )(total, before, after, *earlier)


def swap_borders(low, high):
    peers = lax.axis_size("fp")
    up = [(i, i + 1) for i in range(peers - 1)]
    down = [(j, i) for i, j in up]
    return lax.ppermute(high, "fp", up), lax.ppermute(low, "fp", down)


def slot_rows(first):
    first = first.reshape(1, GROUPS * MOST)
    blocks = [first]
    for k in range(1, VISITS):
        blocks.append(lax.ppermute(first, "visit", [(i, (i + k) % VISITS) for i in range(VISITS)]))
    first = jnp.concatenate(blocks).astype(jnp.int32)
    rows = first[:, :, None] + jnp.arange(PIECE_ROWS, dtype=jnp.int32)
    return rows.reshape(VISITS, 1, GROUPS * MOST * PIECE_ROWS)


def shards(
    image,
    inv_var,
    bg_grid,
    bg_mix,
    psf_taps,
    warp_shift,
    bad_cols,
    piece_patch,
    piece_pos,
    band_of_visit,
):
    where = jnp.stack([lax.axis_index("visit"), lax.axis_index("fp")]).astype(jnp.int32)
    patches = piece_patch[0, :, 0]
    packed = pack(where, bg_mix, patches, piece_pos, bg_grid)
    packed = lax.all_to_all(packed, "fp", split_axis=0, concat_axis=0, tiled=True)
    common = (psf_taps, warp_shift, patches, bad_cols)
    chunks = range(SPAN // WIDTH)
    weights, arrived = [], []
    for chunk in chunks:
        pieces, weight = send_weight(chunk, *common, inv_var)
        weights.append(weight)
        arrived.append(exchange(pieces))
    for chunk in chunks:
        arrived.append(
            exchange(send_flux(chunk, *common, image, packed, weights[chunk]))
        )
    dest_rows = slot_rows(packed[:, GRID_ROWS, :MOST])
    outs = [[], []]
    for turn, received in enumerate(arrived):
        total, low, high = scatter(where, band_of_visit, dest_rows, received)
        kind, chunk = divmod(turn, len(chunks))
        outs[kind] = [merge(chunk, total, *swap_borders(low, high), outs[kind])]
    return (outs[1][0][:, None], outs[0][0][:, None])


def solution(mesh):
    placed = (
        P("visit", "fp", None),
        P("visit", "fp", None),
        P("visit", "fp", None, None),
        P(),
        P("visit", "fp", None),
        P("visit", "fp"),
        P("fp", None),
        P("visit", "fp", None),
        P("visit", "fp"),
        P(),
    )
    return jax.shard_map(
        shards,
        mesh=mesh,
        in_specs=placed,
        out_specs=(P(None, "fp", None, "visit"), P(None, "fp", None, "visit")),
        check_vma=False,
    )
```

```python
import functools

import jax
import jax.numpy as jnp
from jax import lax
from jax.experimental import pallas as pl
from jax.experimental.pallas import tpu as pltpu
from jax.sharding import PartitionSpec as P

ROW_PIX = 4096
BANDS = 4
CCD_ROWS = 256
MOST = 2
BORDER = 100
EDGE = 2 * BORDER
TAPS_HALF = 10
FRAME = 456
HALF = 16
TAPS = 2 * HALF + 1
PIECES = 16
PIECE_ROWS = 16
BINS = 128
BIN_PIX = ROW_PIX // BINS
PATCHES = 16
VISITS = 8
GROUPS = 16
GRID_ROWS = 16
PACKED = GRID_ROWS + 8
BAD_COUNT = 32
AT_SLOT = 0
AT_BAD = 16
AT_SHIFT = 48
AT_VISIT = 49
AT_ORDER = 56
SPAN = ROW_PIX // VISITS
CHUNKS = 1
LIM = 60
BLOCK = 256
PAD = 128
WINDOW = BLOCK + 2 * PAD
UNUSED = 1 << 20
WIDTH = SPAN // CHUNKS


def fill_band(table_ref, psf_ref, band_ref, absolute):
    shape = (16, WINDOW)
    step = lax.broadcasted_iota(jnp.int32, shape, 0) - 2
    lag = 3 * PAD - lax.broadcasted_iota(jnp.int32, shape, 1) - step
    offset = (table_ref[0, AT_SHIFT] - 16 * step).astype(jnp.float32) / 16.0
    angle = offset * jnp.float32(jnp.pi)
    safe = jnp.where(offset == 0.0, 1.0, angle)
    lanczos = jnp.where(
        offset == 0.0, 1.0, 3.0 * jnp.sin(safe) * jnp.sin(safe / 3.0) / (safe * safe)
    )
    lanczos = jnp.where((jnp.abs(offset) < 3.0) & (step < 7), lanczos, 0.0)
    lanczos = lanczos / jnp.sum(lanczos, axis=0, keepdims=True)
    taps = jnp.zeros(shape, jnp.float32)
    total = psf_ref[0, 0]
    for e in range(2 * TAPS_HALF + 1):
        value = psf_ref[0, e]
        taps = jnp.where(lag == e - TAPS_HALF, value, taps)
        total = total + value if e else total
    combined = jnp.sum(lanczos * (taps / total), axis=0, keepdims=True)
    combined = jnp.abs(combined) if absolute else combined
    rolled = pltpu.roll(
        jnp.broadcast_to(combined, (128, WINDOW)), 0, axis=1, stride=1, stride_axis=0
    ).astype(jnp.bfloat16)
    for i in range(WINDOW // 128):
        for o in range(BLOCK // 128):
            tile = (o - i) % (WINDOW // 128)
            band_ref[128 * i : 128 * (i + 1), 128 * o : 128 * (o + 1)] = rolled[
                :, 128 * tile : 128 * (tile + 1)
            ]


def fill_good(table_ref, good_ref):
    columns = lax.broadcasted_iota(jnp.int32, good_ref.shape, 1) - PAD
    good = (columns >= 0) & (columns < ROW_PIX)
    for k in range(BAD_COUNT):
        good = good & (columns != table_ref[0, AT_BAD + k])
    good_ref[...] = good.astype(jnp.float32)


def convolve(window, band_ref, width):
    parts = [
        jnp.dot(
            window[:, BLOCK * n : BLOCK * n + WINDOW],
            band_ref[...],
            preferred_element_type=jnp.float32,
        )
        for n in range(width // BLOCK)
    ]
    return parts[0] if len(parts) == 1 else jnp.concatenate(parts, axis=1)


def send_pieces(table_ref, out_ref, values):
    out_ref[...] = jnp.zeros(out_ref.shape, out_ref.dtype)
    for j in range(PIECES):
        out_ref[0, table_ref[0, AT_SLOT + j]] = values[PIECE_ROWS * j : PIECE_ROWS * (j + 1)]


def pack_body(
    mix_ref, patch_ref, pos_ref, psf_ref, shift_ref, bad_ref, band_ref, grid_ref, out_ref, table_ref, taps_ref
):
    group = lax.axis_index("fp")
    shape = (PATCHES, BINS)
    patch = lax.broadcasted_iota(jnp.int32, shape, 0)
    slot = lax.broadcasted_iota(jnp.int32, shape, 1)
    lane = lax.broadcasted_iota(jnp.int32, (1, BINS), 1)
    first = jnp.full(shape, UNUSED, jnp.int32)
    patches = [patch_ref[j] for j in range(PIECES)]
    table = jnp.zeros((1, BINS), jnp.int32)
    for j in range(PIECES):
        rank = jnp.int32(0)
        for k in range(j):
            rank = rank + (patches[k] == patches[j]).astype(jnp.int32)
        first = jnp.where((patch == patches[j]) & (slot == rank), pos_ref[0, j], first)
        table = jnp.where(
            lane == AT_SLOT + j, patches[j] * MOST + jnp.minimum(rank, MOST - 1), table
        )
    first = first.astype(jnp.float32)
    for q in range(PATCHES):
        out_ref[q, :GRID_ROWS] = grid_ref[0, 0] * mix_ref[q, group]
        out_ref[q, GRID_ROWS:] = jnp.broadcast_to(first[q : q + 1], (PACKED - GRID_ROWS, BINS))
    for k in range(BAD_COUNT):
        table = jnp.where(lane == AT_BAD + k, bad_ref[0, k], table)
    table = jnp.where(lane == AT_SHIFT, shift_ref[0, 0], table)
    table = jnp.where(lane == AT_VISIT, lax.axis_index("visit"), table)
    bands = [band_ref[v] for v in range(VISITS)]
    for v in range(VISITS):
        place = bands[v] * (VISITS // BANDS)
        for u in range(v):
            place = place + (bands[u] == bands[v]).astype(jnp.int32)
        table = jnp.where(lane == AT_ORDER + place, v, table)
    table_ref[...] = table
    taps = jnp.zeros((1, BINS), jnp.float32)
    for e in range(2 * TAPS_HALF + 1):
        taps = jnp.where(lane == e, psf_ref[0, 0, e], taps)
    taps_ref[...] = taps


def masked_window(chunk, good_ref, left_ref, mid_ref, right_ref):
    width = mid_ref.shape[-1]
    start = pl.multiple_of(pl.program_id(0) * SPAN + chunk * width, 128)
    good = good_ref[:, pl.ds(start, width + 2 * PAD)]
    window = jnp.concatenate([left_ref[0], mid_ref[0], right_ref[0]], axis=1)
    return start, good, window * good.astype(jnp.bfloat16)


def weight_body(
    chunk,
    table_ref,
    psf_ref,
    left_ref,
    mid_ref,
    right_ref,
    send_ref,
    weight_ref,
    good_ref,
    band_ref,
):
    @pl.when(pl.program_id(0) == 0)
    def _():
        fill_good(table_ref, good_ref)
        fill_band(table_ref, psf_ref, band_ref, True)

    _, _, window = masked_window(chunk, good_ref, left_ref, mid_ref, right_ref)
    weight = convolve(window, band_ref, mid_ref.shape[-1]).astype(jnp.bfloat16)
    weight_ref[0] = weight
    send_pieces(table_ref, send_ref, weight)


def flux_body(
    chunk,
    table_ref,
    psf_ref,
    left_ref,
    mid_ref,
    right_ref,
    packed_ref,
    weight_ref,
    send_ref,
    good_ref,
    band_ref,
    model_ref,
):
    @pl.when(pl.program_id(0) == 0)
    def _():
        fill_good(table_ref, good_ref)
        fill_band(table_ref, psf_ref, band_ref, False)
        model = packed_ref[0, :GRID_ROWS]
        for k in range(1, GROUPS):
            model = model + packed_ref[k, :GRID_ROWS]
        upper = model.astype(jnp.bfloat16)
        model_ref[:GRID_ROWS] = upper
        model_ref[GRID_ROWS:] = (model - upper.astype(jnp.float32)).astype(jnp.bfloat16)

    width = mid_ref.shape[-1]
    start, good, window = masked_window(chunk, good_ref, left_ref, mid_ref, right_ref)
    shape = (BINS, width + 2 * PAD)
    first = lax.broadcasted_iota(jnp.int32, shape, 0) * BIN_PIX
    column = lax.broadcasted_iota(jnp.int32, shape, 1) + (start - PAD)
    spread = ((column >= first) & (column < first + BIN_PIX)).astype(jnp.bfloat16)
    expanded = jnp.dot(model_ref[...], spread, preferred_element_type=jnp.float32) * good
    warped = convolve(
        jnp.concatenate([window, expanded.astype(jnp.bfloat16)], axis=0), band_ref, width
    )
    backdrop = warped[CCD_ROWS : CCD_ROWS + GRID_ROWS] + warped[CCD_ROWS + GRID_ROWS :]
    backdrop = jnp.broadcast_to(
        backdrop[:, None, :], (GRID_ROWS, CCD_ROWS // GRID_ROWS, width)
    ).reshape(CCD_ROWS, width)
    flux = warped[:CCD_ROWS] - backdrop
    send_pieces(
        table_ref, send_ref, (flux * weight_ref[0].astype(jnp.float32)).astype(jnp.bfloat16)
    )


def scatter_body(table_ref, rows_ref, received_ref, total_ref, low_ref, high_ref):
    turn = pl.program_id(1)
    slots = rows_ref.shape[-1]
    place = lax.broadcasted_iota(jnp.int32, (FRAME, slots), 0) == rows_ref[0]
    frames = jnp.dot(
        place.astype(jnp.bfloat16), received_ref[0], preferred_element_type=jnp.float32
    )

    @pl.when(turn == 0)
    def _():
        total_ref[0] = frames

    @pl.when(turn == 1)
    def _():
        total = total_ref[0] + frames
        total_ref[0] = total
        low_ref[0] = total[:EDGE].astype(jnp.bfloat16)
        high_ref[0] = total[FRAME - EDGE :].astype(jnp.bfloat16)


def merge_body(total_ref, before_ref, after_ref, *refs):
    out_ref = refs[-1]
    total = total_ref[0]
    out_ref[0, :EDGE] = total[:EDGE] + before_ref[0].astype(jnp.float32)
    out_ref[0, EDGE : FRAME - EDGE] = total[EDGE : FRAME - EDGE]
    out_ref[0, FRAME - EDGE :] = total[FRAME - EDGE :] + after_ref[0].astype(jnp.float32)


SMEM = pl.BlockSpec(memory_space=pltpu.SMEM)


def whole(shape):
    zeros = (0,) * len(shape)
    return pl.BlockSpec(shape, lambda i, *_: zeros)


def params(mebibytes):
    return pltpu.CompilerParams(
        dimension_semantics=("arbitrary",), vmem_limit_bytes=mebibytes << 20
    )


def window_specs(chunk):
    per = SPAN // WIDTH
    tiles = WIDTH // 128
    last = ROW_PIX // 128 - 1
    left = pl.BlockSpec(
        (1, CCD_ROWS, 128),
        lambda i, *_: (0, 0, jnp.maximum((per * i + chunk) * tiles - 1, 0)),
    )
    mid = pl.BlockSpec((1, CCD_ROWS, WIDTH), lambda i, *_: (0, 0, per * i + chunk))
    right = pl.BlockSpec(
        (1, CCD_ROWS, 128),
        lambda i, *_: (0, 0, jnp.minimum((per * i + chunk + 1) * tiles, last)),
    )
    return [left, mid, right]


SEND_SHAPE = (VISITS, PATCHES * MOST, PIECE_ROWS, WIDTH)
SEND_BLOCK = pl.BlockSpec((1,) + SEND_SHAPE[1:], lambda i, *_: (i, 0, 0, 0))
WEIGHT_BLOCK = pl.BlockSpec((1, CCD_ROWS, WIDTH), lambda i, *_: (i, 0, 0))
GOOD_SCRATCH = pltpu.VMEM((1, ROW_PIX + 2 * PAD), jnp.float32)
BAND_SCRATCH = pltpu.VMEM((WINDOW, BLOCK), jnp.bfloat16)


def send_weight(chunk, table, psf, inv_var):
    return pl.pallas_call(
        functools.partial(weight_body, chunk),
        grid=(VISITS,),
        in_specs=[SMEM] * 2 + window_specs(chunk),
        out_specs=[SEND_BLOCK, WEIGHT_BLOCK],
        out_shape=[
            jax.ShapeDtypeStruct(SEND_SHAPE, jnp.bfloat16),
            jax.ShapeDtypeStruct((VISITS, CCD_ROWS, WIDTH), jnp.bfloat16),
        ],
        scratch_shapes=[GOOD_SCRATCH, BAND_SCRATCH],
        compiler_params=params(LIM),
        name="send_weight",
    )(table, psf, inv_var, inv_var, inv_var)


def pack(*smalls):
    return pl.pallas_call(
        pack_body,
        in_specs=[SMEM] * (len(smalls) - 1) + [pl.BlockSpec(memory_space=pltpu.VMEM)],
        out_specs=[pl.BlockSpec(memory_space=pltpu.VMEM)] * 3,
        out_shape=[
            jax.ShapeDtypeStruct((PATCHES, PACKED, BINS), jnp.float32),
            jax.ShapeDtypeStruct((1, BINS), jnp.int32),
            jax.ShapeDtypeStruct((1, BINS), jnp.float32),
        ],
        name="pack",
    )(*smalls)


def send_flux(chunk, table, psf, image, packed, weight):
    return pl.pallas_call(
        functools.partial(flux_body, chunk),
        grid=(VISITS,),
        in_specs=[SMEM] * 2 + window_specs(chunk) + [whole(packed.shape), WEIGHT_BLOCK],
        out_specs=SEND_BLOCK,
        out_shape=jax.ShapeDtypeStruct(SEND_SHAPE, jnp.bfloat16),
        scratch_shapes=[
            GOOD_SCRATCH,
            BAND_SCRATCH,
            pltpu.VMEM((2 * GRID_ROWS, BINS), jnp.bfloat16),
        ],
        compiler_params=params(LIM),
        name="send_flux",
    )(table, psf, image, image, image, packed, weight)


def exchange(pieces):
    sent = pieces.reshape(VISITS * PATCHES, MOST, PIECE_ROWS, WIDTH)
    return lax.all_to_all(sent, ("visit", "fp"), split_axis=0, concat_axis=0, tiled=True)


def scatter(table, dest_rows, received):
    slots = PATCHES * MOST * PIECE_ROWS
    shapes = [
        jax.ShapeDtypeStruct((BANDS, FRAME, WIDTH), jnp.float32),
        jax.ShapeDtypeStruct((BANDS, EDGE, WIDTH), jnp.bfloat16),
        jax.ShapeDtypeStruct((BANDS, EDGE, WIDTH), jnp.bfloat16),
    ]
    turns = VISITS // BANDS

    def visit(b, j, at):
        return at[0, AT_ORDER + turns * b + j]

    return pl.pallas_call(
        scatter_body,
        grid_spec=pltpu.PrefetchScalarGridSpec(
            num_scalar_prefetch=1,
            grid=(BANDS, turns),
            in_specs=[
                pl.BlockSpec(
                    (1, 1, slots),
                    lambda b, j, at: ((at[0, AT_VISIT] - visit(b, j, at)) & (VISITS - 1), 0, 0),
                ),
                pl.BlockSpec((1, slots, WIDTH), lambda b, j, at: (visit(b, j, at), 0, 0)),
            ],
            out_specs=[
                pl.BlockSpec((1,) + shape.shape[1:], lambda b, j, at: (b, 0, 0)) for shape in shapes
            ],
        ),
        out_shape=shapes,
        compiler_params=pltpu.CompilerParams(
            dimension_semantics=("arbitrary", "arbitrary"), vmem_limit_bytes=16 << 20
        ),
        name="scatter",
    )(table, dest_rows, received.reshape(VISITS, slots, WIDTH))


def merge(chunk, total, before, after, earlier):
    edge = pl.BlockSpec((1, EDGE, WIDTH), lambda i: (i, 0, 0))
    frame = pl.BlockSpec((1, FRAME, WIDTH), lambda i: (i, 0, 0))
    return pl.pallas_call(
        merge_body,
        grid=(BANDS,),
        in_specs=[frame, edge, edge] + [pl.BlockSpec(memory_space=pl.ANY)] * len(earlier),
        out_specs=pl.BlockSpec((1, FRAME, WIDTH), lambda i: (i, 0, chunk)),
        out_shape=jax.ShapeDtypeStruct((BANDS, FRAME, SPAN), jnp.float32),
        input_output_aliases={3: 0} if earlier else {},
        compiler_params=params(16),
        name="merge",
    )(total, before, after, *earlier)


def swap_borders(low, high):
    peers = lax.axis_size("fp")
    up = [(i, i + 1) for i in range(peers - 1)]
    down = [(j, i) for i, j in up]
    return lax.ppermute(high, "fp", up), lax.ppermute(low, "fp", down)


def slot_rows(first):
    first = first.reshape(1, GROUPS * MOST)
    blocks = [first]
    for k in range(1, VISITS):
        blocks.append(lax.ppermute(first, "visit", [(i, (i + k) % VISITS) for i in range(VISITS)]))
    first = jnp.concatenate(blocks).astype(jnp.int32)
    rows = first[:, :, None] + jnp.arange(PIECE_ROWS, dtype=jnp.int32)
    return rows.reshape(VISITS, 1, GROUPS * MOST * PIECE_ROWS)


def shards(
    image,
    inv_var,
    bg_grid,
    bg_mix,
    psf_taps,
    warp_shift,
    bad_cols,
    piece_patch,
    piece_pos,
    band_of_visit,
):
    packed, table, psf = pack(
        bg_mix,
        piece_patch[0, :, 0],
        piece_pos,
        psf_taps,
        warp_shift,
        bad_cols,
        band_of_visit,
        bg_grid,
    )
    packed = lax.all_to_all(packed, "fp", split_axis=0, concat_axis=0, tiled=True)
    chunks = range(SPAN // WIDTH)
    weights, arrived = [], []
    for chunk in chunks:
        pieces, weight = send_weight(chunk, table, psf, inv_var)
        weights.append(weight)
        arrived.append(exchange(pieces))
    fluxes = [send_flux(chunk, table, psf, image, packed, weights[chunk]) for chunk in chunks]
    dest_rows = slot_rows(packed[:, GRID_ROWS, :MOST])
    fluxes, dest_rows = lax.optimization_barrier((fluxes, dest_rows))
    arrived += [exchange(pieces) for pieces in fluxes]
    outs = [[], []]
    for turn, received in enumerate(arrived):
        total, low, high = scatter(table, dest_rows, received)
        kind, chunk = divmod(turn, len(chunks))
        outs[kind] = [merge(chunk, total, *swap_borders(low, high), outs[kind])]
    return (outs[1][0][:, None], outs[0][0][:, None])


def solution(mesh):
    placed = (
        P("visit", "fp", None),
        P("visit", "fp", None),
        P("visit", "fp", None, None),
        P(),
        P("visit", "fp", None),
        P("visit", "fp"),
        P("fp", None),
        P("visit", "fp", None),
        P("visit", "fp"),
        P(),
    )
    return jax.shard_map(
        shards,
        mesh=mesh,
        in_specs=placed,
        out_specs=(P(None, "fp", None, "visit"), P(None, "fp", None, "visit")),
        check_vma=False,
    )
```

```python
import functools

import jax
import jax.numpy as jnp
from jax import lax
from jax.experimental import pallas as pl
from jax.experimental.pallas import tpu as pltpu
from jax.sharding import PartitionSpec as P

ROW_PIX = 4096
BANDS = 4
CCD_ROWS = 256
MOST = 2
BORDER = 100
EDGE = 2 * BORDER
TAPS_HALF = 10
FRAME = 456
HALF = 16
TAPS = 2 * HALF + 1
PIECES = 16
PIECE_ROWS = 16
BINS = 128
BIN_PIX = ROW_PIX // BINS
PATCHES = 16
VISITS = 8
TURNS = VISITS // BANDS
GROUPS = 16
GRID_ROWS = 16
PACKED = GRID_ROWS + 8
BAD_COUNT = 32
AT_SLOT = 0
AT_BAD = 16
AT_SHIFT = 48
AT_VISIT = 49
AT_ORDER = 56
SPAN = ROW_PIX // VISITS
PER = 4
HALVES = 2
BLOCK = 256
PAD = 128
WINDOW = BLOCK + 2 * PAD
UNUSED = 1 << 20
STEPS = VISITS // PER
WIDTH = SPAN * PER


def fill_band(table_ref, psf_ref, band_ref, absolute):
    shape = (16, WINDOW)
    step = lax.broadcasted_iota(jnp.int32, shape, 0) - 2
    lag = 3 * PAD - lax.broadcasted_iota(jnp.int32, shape, 1) - step
    offset = (table_ref[0, AT_SHIFT] - 16 * step).astype(jnp.float32) / 16.0
    angle = offset * jnp.float32(jnp.pi)
    safe = jnp.where(offset == 0.0, 1.0, angle)
    lanczos = jnp.where(
        offset == 0.0, 1.0, 3.0 * jnp.sin(safe) * jnp.sin(safe / 3.0) / (safe * safe)
    )
    lanczos = jnp.where((jnp.abs(offset) < 3.0) & (step < 7), lanczos, 0.0)
    lanczos = lanczos / jnp.sum(lanczos, axis=0, keepdims=True)
    taps = jnp.zeros(shape, jnp.float32)
    total = psf_ref[0, 0]
    for e in range(2 * TAPS_HALF + 1):
        value = psf_ref[0, e]
        taps = jnp.where(lag == e - TAPS_HALF, value, taps)
        total = total + value if e else total
    combined = jnp.sum(lanczos * (taps / total), axis=0, keepdims=True)
    combined = jnp.abs(combined) if absolute else combined
    rolled = pltpu.roll(
        jnp.broadcast_to(combined, (128, WINDOW)), 0, axis=1, stride=1, stride_axis=0
    ).astype(jnp.bfloat16)
    for i in range(WINDOW // 128):
        for o in range(BLOCK // 128):
            tile = (o - i) % (WINDOW // 128)
            band_ref[128 * i : 128 * (i + 1), 128 * o : 128 * (o + 1)] = rolled[
                :, 128 * tile : 128 * (tile + 1)
            ]


def fill_good(table_ref, good_ref):
    columns = lax.broadcasted_iota(jnp.int32, good_ref.shape, 1) - PAD
    good = (columns >= 0) & (columns < ROW_PIX)
    for k in range(BAD_COUNT):
        good = good & (columns != table_ref[0, AT_BAD + k])
    good_ref[...] = good.astype(jnp.float32)


def convolve(window, band_ref, span):
    parts = [
        jnp.dot(
            window[:, start : start + WINDOW], band_ref[...], preferred_element_type=jnp.float32
        )
        for start in range(span * SPAN, (span + 1) * SPAN, BLOCK)
    ]
    return jnp.concatenate(parts, axis=1)


def send_pieces(table_ref, out_ref, span, values):
    out_ref[span] = jnp.zeros(out_ref.shape[1:], out_ref.dtype)
    for j in range(PIECES):
        out_ref[span, table_ref[0, AT_SLOT + j]] = values[PIECE_ROWS * j : PIECE_ROWS * (j + 1)]


def pack_body(
    mix_ref, patch_ref, pos_ref, psf_ref, shift_ref, bad_ref, band_ref, grid_ref, out_ref, table_ref, taps_ref
):
    group = lax.axis_index("fp")
    shape = (PATCHES, BINS)
    patch = lax.broadcasted_iota(jnp.int32, shape, 0)
    slot = lax.broadcasted_iota(jnp.int32, shape, 1)
    lane = lax.broadcasted_iota(jnp.int32, (1, BINS), 1)
    first = jnp.full(shape, UNUSED, jnp.int32)
    patches = [patch_ref[j] for j in range(PIECES)]
    table = jnp.zeros((1, BINS), jnp.int32)
    for j in range(PIECES):
        rank = jnp.int32(0)
        for k in range(j):
            rank = rank + (patches[k] == patches[j]).astype(jnp.int32)
        first = jnp.where((patch == patches[j]) & (slot == rank), pos_ref[0, j], first)
        table = jnp.where(
            lane == AT_SLOT + j, patches[j] * MOST + jnp.minimum(rank, MOST - 1), table
        )
    first = first.astype(jnp.float32)
    for q in range(PATCHES):
        out_ref[q, :GRID_ROWS] = grid_ref[0, 0] * mix_ref[q, group]
        out_ref[q, GRID_ROWS:] = jnp.broadcast_to(first[q : q + 1], (PACKED - GRID_ROWS, BINS))
    for k in range(BAD_COUNT):
        table = jnp.where(lane == AT_BAD + k, bad_ref[0, k], table)
    table = jnp.where(lane == AT_SHIFT, shift_ref[0, 0], table)
    table = jnp.where(lane == AT_VISIT, lax.axis_index("visit"), table)
    bands = [band_ref[v] for v in range(VISITS)]
    for v in range(VISITS):
        place = bands[v] * TURNS
        for u in range(v):
            place = place + (bands[u] == bands[v]).astype(jnp.int32)
        table = jnp.where(lane == AT_ORDER + place, v, table)
    table_ref[...] = table
    taps = jnp.zeros((1, BINS), jnp.float32)
    for e in range(2 * TAPS_HALF + 1):
        taps = jnp.where(lane == e, psf_ref[0, 0, e], taps)
    taps_ref[...] = taps


def masked_window(good_ref, left_ref, mid_ref, right_ref):
    start = pl.multiple_of(pl.program_id(0) * WIDTH, 128)
    good = good_ref[:, pl.ds(start, WIDTH + 2 * PAD)]
    window = jnp.concatenate([left_ref[0], mid_ref[0], right_ref[0]], axis=1)
    return start, good, window * good.astype(jnp.bfloat16)


def weight_body(
    table_ref,
    psf_ref,
    left_ref,
    mid_ref,
    right_ref,
    send_ref,
    weight_ref,
    good_ref,
    band_ref,
):
    @pl.when(pl.program_id(0) == 0)
    def _():
        fill_good(table_ref, good_ref)
        fill_band(table_ref, psf_ref, band_ref, True)

    _, _, window = masked_window(good_ref, left_ref, mid_ref, right_ref)
    for span in range(PER):
        weight = convolve(window, band_ref, span).astype(jnp.bfloat16)
        weight_ref[span] = weight
        send_pieces(table_ref, send_ref, span, weight)


def flux_body(
    table_ref,
    psf_ref,
    left_ref,
    mid_ref,
    right_ref,
    packed_ref,
    weight_ref,
    send_ref,
    good_ref,
    band_ref,
    model_ref,
):
    @pl.when(pl.program_id(0) == 0)
    def _():
        fill_good(table_ref, good_ref)
        fill_band(table_ref, psf_ref, band_ref, False)
        model = packed_ref[0, :GRID_ROWS]
        for k in range(1, GROUPS):
            model = model + packed_ref[k, :GRID_ROWS]
        upper = model.astype(jnp.bfloat16)
        model_ref[:GRID_ROWS] = upper
        model_ref[GRID_ROWS:] = (model - upper.astype(jnp.float32)).astype(jnp.bfloat16)

    start, good, window = masked_window(good_ref, left_ref, mid_ref, right_ref)
    shape = (BINS, WIDTH + 2 * PAD)
    first = lax.broadcasted_iota(jnp.int32, shape, 0) * BIN_PIX
    column = lax.broadcasted_iota(jnp.int32, shape, 1) + (start - PAD)
    spread = ((column >= first) & (column < first + BIN_PIX)).astype(jnp.bfloat16)
    expanded = jnp.dot(model_ref[...], spread, preferred_element_type=jnp.float32) * good
    window = jnp.concatenate([window, expanded.astype(jnp.bfloat16)], axis=0)
    for span in range(PER):
        warped = convolve(window, band_ref, span)
        backdrop = warped[CCD_ROWS : CCD_ROWS + GRID_ROWS] + warped[CCD_ROWS + GRID_ROWS :]
        backdrop = jnp.broadcast_to(
            backdrop[:, None, :], (GRID_ROWS, CCD_ROWS // GRID_ROWS, SPAN)
        ).reshape(CCD_ROWS, SPAN)
        flux = warped[:CCD_ROWS] - backdrop
        product = flux * weight_ref[span].astype(jnp.float32)
        send_pieces(table_ref, send_ref, span, product.astype(jnp.bfloat16))


def scatter_body(half, table_ref, rows_ref, *refs):
    received_refs, (total_ref, low_ref, high_ref) = refs[:TURNS], refs[TURNS:]
    slots = rows_ref.shape[-1]
    total = None
    for turn, received_ref in enumerate(received_refs):
        visit = table_ref[0, AT_ORDER + TURNS * (half + pl.program_id(0)) + turn]
        rows = rows_ref[(table_ref[0, AT_VISIT] - visit) & (VISITS - 1)]
        place = lax.broadcasted_iota(jnp.int32, (FRAME, slots), 0) == rows
        frames = jnp.dot(
            place.astype(jnp.bfloat16), received_ref[0], preferred_element_type=jnp.float32
        )
        total = total + frames if turn else frames
    total_ref[0] = total
    low_ref[0] = total[:EDGE].astype(jnp.bfloat16)
    high_ref[0] = total[FRAME - EDGE :].astype(jnp.bfloat16)


def merge_body(total_ref, before_ref, after_ref, *refs):
    out_ref = refs[-1]
    total = total_ref[0]
    out_ref[0, :EDGE] = total[:EDGE] + before_ref[0].astype(jnp.float32)
    out_ref[0, EDGE : FRAME - EDGE] = total[EDGE : FRAME - EDGE]
    out_ref[0, FRAME - EDGE :] = total[FRAME - EDGE :] + after_ref[0].astype(jnp.float32)


SMEM = pl.BlockSpec(memory_space=pltpu.SMEM)


def whole(shape):
    zeros = (0,) * len(shape)
    return pl.BlockSpec(shape, lambda i, *_: zeros)


def params(mebibytes):
    return pltpu.CompilerParams(
        dimension_semantics=("arbitrary",), vmem_limit_bytes=mebibytes << 20
    )


def window_specs():
    tiles = WIDTH // 128
    last = ROW_PIX // 128 - 1
    left = pl.BlockSpec((1, CCD_ROWS, 128), lambda i: (0, 0, jnp.maximum(i * tiles - 1, 0)))
    mid = pl.BlockSpec((1, CCD_ROWS, WIDTH), lambda i: (0, 0, i))
    right = pl.BlockSpec((1, CCD_ROWS, 128), lambda i: (0, 0, jnp.minimum((i + 1) * tiles, last)))
    return [left, mid, right]


SEND_SHAPE = (VISITS, PATCHES * MOST, PIECE_ROWS, SPAN)
SEND_BLOCK = pl.BlockSpec((PER,) + SEND_SHAPE[1:], lambda i: (i, 0, 0, 0))
WEIGHT_BLOCK = pl.BlockSpec((PER, CCD_ROWS, SPAN), lambda i: (i, 0, 0))
GOOD_SCRATCH = pltpu.VMEM((1, ROW_PIX + 2 * PAD), jnp.float32)
BAND_SCRATCH = pltpu.VMEM((WINDOW, BLOCK), jnp.bfloat16)


def send_weight(table, psf, inv_var):
    return pl.pallas_call(
        weight_body,
        grid=(STEPS,),
        in_specs=[SMEM] * 2 + window_specs(),
        out_specs=[SEND_BLOCK, WEIGHT_BLOCK],
        out_shape=[
            jax.ShapeDtypeStruct(SEND_SHAPE, jnp.bfloat16),
            jax.ShapeDtypeStruct((VISITS, CCD_ROWS, SPAN), jnp.bfloat16),
        ],
        scratch_shapes=[GOOD_SCRATCH, BAND_SCRATCH],
        compiler_params=params(60),
        name="send_weight",
    )(table, psf, inv_var, inv_var, inv_var)


def pack(*smalls):
    return pl.pallas_call(
        pack_body,
        in_specs=[SMEM] * (len(smalls) - 1) + [pl.BlockSpec(memory_space=pltpu.VMEM)],
        out_specs=[pl.BlockSpec(memory_space=pltpu.VMEM)] * 3,
        out_shape=[
            jax.ShapeDtypeStruct((PATCHES, PACKED, BINS), jnp.float32),
            jax.ShapeDtypeStruct((1, BINS), jnp.int32),
            jax.ShapeDtypeStruct((1, BINS), jnp.float32),
        ],
        name="pack",
    )(*smalls)


def send_flux(table, psf, image, packed, weight):
    return pl.pallas_call(
        flux_body,
        grid=(STEPS,),
        in_specs=[SMEM] * 2 + window_specs() + [whole(packed.shape), WEIGHT_BLOCK],
        out_specs=SEND_BLOCK,
        out_shape=jax.ShapeDtypeStruct(SEND_SHAPE, jnp.bfloat16),
        scratch_shapes=[
            GOOD_SCRATCH,
            BAND_SCRATCH,
            pltpu.VMEM((2 * GRID_ROWS, BINS), jnp.bfloat16),
        ],
        compiler_params=params(60),
        name="send_flux",
    )(table, psf, image, image, image, packed, weight)


def exchange(pieces):
    sent = pieces.reshape(VISITS * PATCHES, MOST, PIECE_ROWS, SPAN)
    return lax.all_to_all(sent, ("visit", "fp"), split_axis=0, concat_axis=0, tiled=True)


def scatter(half, table, dest_rows, received):
    slots = PATCHES * MOST * PIECE_ROWS
    bands = BANDS // HALVES
    shapes = [
        jax.ShapeDtypeStruct((bands, FRAME, SPAN), jnp.float32),
        jax.ShapeDtypeStruct((bands, EDGE, SPAN), jnp.bfloat16),
        jax.ShapeDtypeStruct((bands, EDGE, SPAN), jnp.bfloat16),
    ]

    def received_spec(turn):
        return pl.BlockSpec(
            (1, slots, SPAN),
            lambda i, at: (at[0, AT_ORDER + TURNS * (bands * half + i) + turn], 0, 0),
        )

    received = received.reshape(VISITS, slots, SPAN)
    return pl.pallas_call(
        functools.partial(scatter_body, bands * half),
        grid_spec=pltpu.PrefetchScalarGridSpec(
            num_scalar_prefetch=1,
            grid=(bands,),
            in_specs=[pl.BlockSpec((VISITS, 1, slots), lambda i, at: (0, 0, 0))]
            + [received_spec(turn) for turn in range(TURNS)],
            out_specs=[
                pl.BlockSpec((1,) + shape.shape[1:], lambda i, at: (i, 0, 0)) for shape in shapes
            ],
        ),
        out_shape=shapes,
        compiler_params=params(16),
        name="scatter",
    )(table, dest_rows, *[received] * TURNS)


def merge(half, total, before, after, earlier):
    bands = BANDS // HALVES
    edge = pl.BlockSpec((1, EDGE, SPAN), lambda i: (i, 0, 0))
    frame = pl.BlockSpec((1, FRAME, SPAN), lambda i: (i, 0, 0))
    return pl.pallas_call(
        merge_body,
        grid=(bands,),
        in_specs=[frame, edge, edge] + [pl.BlockSpec(memory_space=pl.ANY)] * len(earlier),
        out_specs=pl.BlockSpec((1, FRAME, SPAN), lambda i: (bands * half + i, 0, 0)),
        out_shape=jax.ShapeDtypeStruct((BANDS, FRAME, SPAN), jnp.float32),
        input_output_aliases={3: 0} if earlier else {},
        compiler_params=params(16),
        name="merge",
    )(total, before, after, *earlier)


def swap_borders(low, high):
    peers = lax.axis_size("fp")
    up = [(i, i + 1) for i in range(peers - 1)]
    down = [(j, i) for i, j in up]
    return lax.ppermute(high, "fp", up), lax.ppermute(low, "fp", down)


def slot_rows(first):
    first = first.reshape(1, GROUPS * MOST)
    blocks = [first]
    for k in range(1, VISITS):
        blocks.append(lax.ppermute(first, "visit", [(i, (i + k) % VISITS) for i in range(VISITS)]))
    first = jnp.concatenate(blocks).astype(jnp.int32)
    rows = first[:, :, None] + jnp.arange(PIECE_ROWS, dtype=jnp.int32)
    return rows.reshape(VISITS, 1, GROUPS * MOST * PIECE_ROWS)


def shards(
    image,
    inv_var,
    bg_grid,
    bg_mix,
    psf_taps,
    warp_shift,
    bad_cols,
    piece_patch,
    piece_pos,
    band_of_visit,
):
    packed, table, psf = pack(
        bg_mix,
        piece_patch[0, :, 0],
        piece_pos,
        psf_taps,
        warp_shift,
        bad_cols,
        band_of_visit,
        bg_grid,
    )
    packed = lax.all_to_all(packed, "fp", split_axis=0, concat_axis=0, tiled=True)
    weight_pieces, weight = send_weight(table, psf, inv_var)
    weight_arrived = exchange(weight_pieces)
    flux_pieces = send_flux(table, psf, image, packed, weight)
    dest_rows = slot_rows(packed[:, GRID_ROWS, :MOST])
    flux_pieces, dest_rows = lax.optimization_barrier((flux_pieces, dest_rows))
    flux_arrived = exchange(flux_pieces)
    outs = []
    for received in (weight_arrived, flux_arrived):
        out = []
        for half in range(HALVES):
            total, low, high = scatter(half, table, dest_rows, received)
            out = [merge(half, total, *swap_borders(low, high), out)]
        outs.append(out[0])
    return (outs[1][:, None], outs[0][:, None])


def solution(mesh):
    placed = (
        P("visit", "fp", None),
        P("visit", "fp", None),
        P("visit", "fp", None, None),
        P(),
        P("visit", "fp", None),
        P("visit", "fp"),
        P("fp", None),
        P("visit", "fp", None),
        P("visit", "fp"),
        P(),
    )
    return jax.shard_map(
        shards,
        mesh=mesh,
        in_specs=placed,
        out_specs=(P(None, "fp", None, "visit"), P(None, "fp", None, "visit")),
        check_vma=False,
    )
```

```python
import jax
import jax.numpy as jnp
from jax import lax
from jax.experimental import pallas as pl
from jax.experimental.pallas import tpu as pltpu
from jax.sharding import PartitionSpec as P

ROW_PIX = 4096
BANDS = 4
CCD_ROWS = 256
TAPS_HALF = 10
FRAME = 456
HALF = 16
PIECES = 16
PIECE_ROWS = 16
BINS = 128
BIN_PIX = ROW_PIX // BINS
PATCHES = 16
VISITS = 8
TURNS = VISITS // BANDS
GROUPS = 16
GRID_ROWS = 16
PACKED = GRID_ROWS + 8
BAD_COUNT = 32
AT_BAD = 16
AT_SHIFT = 48
AT_VISIT = 49
AT_ORDER = 56
SPAN = ROW_PIX // VISITS
PER = 4
PARTS = 4
LANES = 128
SHARE = LANES // PARTS
PART_ROWS = CCD_ROWS // PARTS
STRIP = 16 * 256 + 208
STRIDE = 256
BLOCK = 256
PAD = 128
WINDOW = BLOCK + 2 * PAD
STEPS = VISITS // PER
WIDTH = SPAN * PER


def fill_band(table_ref, psf_ref, band_ref, absolute):
    shape = (16, WINDOW)
    step = lax.broadcasted_iota(jnp.int32, shape, 0) - 2
    lag = 3 * PAD - lax.broadcasted_iota(jnp.int32, shape, 1) - step
    offset = (table_ref[0, AT_SHIFT] - 16 * step).astype(jnp.float32) / 16.0
    angle = offset * jnp.float32(jnp.pi)
    safe = jnp.where(offset == 0.0, 1.0, angle)
    lanczos = jnp.where(
        offset == 0.0, 1.0, 3.0 * jnp.sin(safe) * jnp.sin(safe / 3.0) / (safe * safe)
    )
    lanczos = jnp.where((jnp.abs(offset) < 3.0) & (step < 7), lanczos, 0.0)
    lanczos = lanczos / jnp.sum(lanczos, axis=0, keepdims=True)
    taps = jnp.zeros(shape, jnp.float32)
    total = psf_ref[0, 0]
    for e in range(2 * TAPS_HALF + 1):
        value = psf_ref[0, e]
        taps = jnp.where(lag == e - TAPS_HALF, value, taps)
        total = total + value if e else total
    combined = jnp.sum(lanczos * (taps / total), axis=0, keepdims=True)
    combined = jnp.abs(combined) if absolute else combined
    rolled = pltpu.roll(
        jnp.broadcast_to(combined, (128, WINDOW)), 0, axis=1, stride=1, stride_axis=0
    ).astype(jnp.bfloat16)
    for i in range(WINDOW // 128):
        for o in range(BLOCK // 128):
            tile = (o - i) % (WINDOW // 128)
            band_ref[128 * i : 128 * (i + 1), 128 * o : 128 * (o + 1)] = rolled[
                :, 128 * tile : 128 * (tile + 1)
            ]


def fill_good(table_ref, good_ref):
    columns = lax.broadcasted_iota(jnp.int32, good_ref.shape, 1) - PAD
    good = (columns >= 0) & (columns < ROW_PIX)
    for k in range(BAD_COUNT):
        good = good & (columns != table_ref[0, AT_BAD + k])
    good_ref[...] = good.astype(jnp.float32)


def convolve(window, band_ref, span):
    parts = [
        jnp.dot(
            window[:, start : start + WINDOW], band_ref[...], preferred_element_type=jnp.float32
        )
        for start in range(span * SPAN, (span + 1) * SPAN, BLOCK)
    ]
    return jnp.concatenate(parts, axis=1)


def lane_part(shape):
    return lax.broadcasted_iota(jnp.int32, shape, 1) // SHARE


def swap_parts(blocks):
    part = lane_part(blocks[0].shape)
    even = part % 2 == 0
    low = part < 2

    def cross(a, b, mask, shift):
        first = jnp.where(mask, a, pltpu.roll(b, shift, axis=1))
        return first, jnp.where(mask, pltpu.roll(a, LANES - shift, axis=1), b)

    y0, y1 = cross(blocks[0], blocks[1], even, SHARE)
    y2, y3 = cross(blocks[2], blocks[3], even, SHARE)
    z0, z2 = cross(y0, y2, low, 2 * SHARE)
    z1, z3 = cross(y1, y3, low, 2 * SHARE)
    return z0, z1, z2, z3


def send_pieces(out_ref, span, values):
    for tile in range(SPAN // LANES):
        column = values[:, LANES * tile : LANES * (tile + 1)]
        blocks = [column[PART_ROWS * g : PART_ROWS * (g + 1)] for g in range(PARTS)]
        for k, block in enumerate(swap_parts(blocks)):
            out_ref[span * (SPAN // SHARE) + PARTS * tile + k] = block.astype(jnp.bfloat16)


def pack_body(
    mix_ref, patch_ref, pos_ref, psf_ref, shift_ref, bad_ref, band_ref, grid_ref, out_ref, table_ref, taps_ref
):
    group = lax.axis_index("fp")
    lane = lax.broadcasted_iota(jnp.int32, (1, BINS), 1)
    table = jnp.zeros((1, BINS), jnp.int32)
    first = table
    for j in range(PIECES):
        first = jnp.where(lane == j, patch_ref[j] * STRIDE + pos_ref[0, j], first)
    first = first.astype(jnp.float32)
    for q in range(PATCHES):
        out_ref[q, :GRID_ROWS] = grid_ref[0, 0] * mix_ref[q, group]
        out_ref[q, GRID_ROWS:] = jnp.broadcast_to(first, (PACKED - GRID_ROWS, BINS))
    for k in range(BAD_COUNT):
        table = jnp.where(lane == AT_BAD + k, bad_ref[0, k], table)
    table = jnp.where(lane == AT_SHIFT, shift_ref[0, 0], table)
    table = jnp.where(lane == AT_VISIT, lax.axis_index("visit"), table)
    bands = [band_ref[v] for v in range(VISITS)]
    for v in range(VISITS):
        place = bands[v] * TURNS
        for u in range(v):
            place = place + (bands[u] == bands[v]).astype(jnp.int32)
        table = jnp.where(lane == AT_ORDER + place, v, table)
    table_ref[...] = table
    taps = jnp.zeros((1, BINS), jnp.float32)
    for e in range(2 * TAPS_HALF + 1):
        taps = jnp.where(lane == e, psf_ref[0, 0, e], taps)
    taps_ref[...] = taps


def masked_window(good_ref, left_ref, mid_ref, right_ref):
    start = pl.multiple_of(pl.program_id(0) * WIDTH, 128)
    good = good_ref[:, pl.ds(start, WIDTH + 2 * PAD)]
    window = jnp.concatenate([left_ref[0], mid_ref[0], right_ref[0]], axis=1)
    return start, good, window * good.astype(jnp.bfloat16)


def weight_body(
    table_ref,
    psf_ref,
    left_ref,
    mid_ref,
    right_ref,
    send_ref,
    weight_ref,
    good_ref,
    band_ref,
):
    @pl.when(pl.program_id(0) == 0)
    def _():
        fill_good(table_ref, good_ref)
        fill_band(table_ref, psf_ref, band_ref, True)

    _, _, window = masked_window(good_ref, left_ref, mid_ref, right_ref)
    for span in range(PER):
        weight = convolve(window, band_ref, span)
        weight_ref[span] = weight.astype(jnp.bfloat16)
        send_pieces(send_ref, span, weight)


def flux_body(
    table_ref,
    psf_ref,
    left_ref,
    mid_ref,
    right_ref,
    packed_ref,
    weight_ref,
    send_ref,
    good_ref,
    band_ref,
    model_ref,
):
    @pl.when(pl.program_id(0) == 0)
    def _():
        fill_good(table_ref, good_ref)
        fill_band(table_ref, psf_ref, band_ref, False)
        model = packed_ref[0, :GRID_ROWS]
        for k in range(1, GROUPS):
            model = model + packed_ref[k, :GRID_ROWS]
        upper = model.astype(jnp.bfloat16)
        model_ref[:GRID_ROWS] = upper
        model_ref[GRID_ROWS:] = (model - upper.astype(jnp.float32)).astype(jnp.bfloat16)

    start, good, window = masked_window(good_ref, left_ref, mid_ref, right_ref)
    shape = (BINS, WIDTH + 2 * PAD)
    first = lax.broadcasted_iota(jnp.int32, shape, 0) * BIN_PIX
    column = lax.broadcasted_iota(jnp.int32, shape, 1) + (start - PAD)
    spread = ((column >= first) & (column < first + BIN_PIX)).astype(jnp.bfloat16)
    expanded = jnp.dot(model_ref[...], spread, preferred_element_type=jnp.float32) * good
    window = jnp.concatenate([window, expanded.astype(jnp.bfloat16)], axis=0)
    for span in range(PER):
        warped = convolve(window, band_ref, span)
        backdrop = warped[CCD_ROWS : CCD_ROWS + GRID_ROWS] + warped[CCD_ROWS + GRID_ROWS :]
        backdrop = jnp.broadcast_to(
            backdrop[:, None, :], (GRID_ROWS, CCD_ROWS // GRID_ROWS, SPAN)
        ).reshape(CCD_ROWS, SPAN)
        flux = warped[:CCD_ROWS] - backdrop
        send_pieces(send_ref, span, flux * weight_ref[span].astype(jnp.float32))


def strip_body(table_ref, rows_ref, received_ref, out_ref, *strips):
    for strip_ref in strips:
        strip_ref[...] = jnp.zeros(strip_ref.shape, strip_ref.dtype)
    part = lane_part((PIECE_ROWS, LANES))
    masks = [part == m for m in range(PARTS)]
    blocks = PART_ROWS // PIECE_ROWS

    def step(index, carry):
        turn = index // (GROUPS * blocks)
        group = index // blocks % GROUPS
        block = index % blocks
        work = []
        for band, strip_ref in enumerate(strips):
            visit = table_ref[0, AT_ORDER + TURNS * band + turn]
            value = received_ref[(visit * GROUPS + group) * blocks + block].astype(jnp.float32)
            base = (((table_ref[0, AT_VISIT] - visit) & (VISITS - 1)) * GROUPS + group) * PIECES
            for m in range(PARTS):
                row = rows_ref[base + blocks * m + block]
                work.append((strip_ref.at[pl.ds(row, PIECE_ROWS), :], value, masks[m]))
        sums = [ref[...] + value for ref, value, _ in work]
        for (ref, _, mask), total in zip(work, sums):
            pltpu.store(ref, total, mask=mask)
        return carry

    lax.fori_loop(0, TURNS * GROUPS * blocks, step, 0)
    part = lane_part((FRAME, LANES))
    even = part % 2 == 0
    low = part < 2

    def fold(a, b, mask, shift):
        return jnp.where(mask, a, b) + pltpu.roll(jnp.where(mask, b, a), shift, axis=1)

    for patch in range(PATCHES):
        frames = [strip_ref[STRIDE * patch : STRIDE * patch + FRAME] for strip_ref in strips]
        first = fold(frames[0], frames[1], even, SHARE)
        second = fold(frames[2], frames[3], even, SHARE)
        out_ref[patch] = fold(first, second, low, 2 * SHARE).astype(jnp.bfloat16)


def spread_body(received_ref, out_ref):
    for tile in range(SPAN // LANES):
        blocks = [received_ref[PARTS * tile + m].astype(jnp.float32) for m in range(PARTS)]
        for band, block in enumerate(swap_parts(blocks)):
            out_ref[band, :, LANES * tile : LANES * (tile + 1)] = block


SMEM = pl.BlockSpec(memory_space=pltpu.SMEM)


def whole(shape):
    zeros = (0,) * len(shape)
    return pl.BlockSpec(shape, lambda i, *_: zeros)


def params(mebibytes):
    return pltpu.CompilerParams(
        dimension_semantics=("arbitrary",), vmem_limit_bytes=mebibytes << 20
    )


def window_specs():
    tiles = WIDTH // 128
    last = ROW_PIX // 128 - 1
    left = pl.BlockSpec((1, CCD_ROWS, 128), lambda i: (0, 0, jnp.maximum(i * tiles - 1, 0)))
    mid = pl.BlockSpec((1, CCD_ROWS, WIDTH), lambda i: (0, 0, i))
    right = pl.BlockSpec((1, CCD_ROWS, 128), lambda i: (0, 0, jnp.minimum((i + 1) * tiles, last)))
    return [left, mid, right]


SEND_SHAPE = (VISITS * GROUPS, PART_ROWS, LANES)
SEND_BLOCK = pl.BlockSpec((PER * GROUPS,) + SEND_SHAPE[1:], lambda i: (i, 0, 0))
WEIGHT_BLOCK = pl.BlockSpec((PER, CCD_ROWS, SPAN), lambda i: (i, 0, 0))
GOOD_SCRATCH = pltpu.VMEM((1, ROW_PIX + 2 * PAD), jnp.float32)
BAND_SCRATCH = pltpu.VMEM((WINDOW, BLOCK), jnp.bfloat16)


def send_weight(table, psf, inv_var):
    return pl.pallas_call(
        weight_body,
        grid=(STEPS,),
        in_specs=[SMEM] * 2 + window_specs(),
        out_specs=[SEND_BLOCK, WEIGHT_BLOCK],
        out_shape=[
            jax.ShapeDtypeStruct(SEND_SHAPE, jnp.bfloat16),
            jax.ShapeDtypeStruct((VISITS, CCD_ROWS, SPAN), jnp.bfloat16),
        ],
        scratch_shapes=[GOOD_SCRATCH, BAND_SCRATCH],
        compiler_params=params(60),
        name="send_weight",
    )(table, psf, inv_var, inv_var, inv_var)


def pack(*smalls):
    return pl.pallas_call(
        pack_body,
        in_specs=[SMEM] * (len(smalls) - 1) + [pl.BlockSpec(memory_space=pltpu.VMEM)],
        out_specs=[pl.BlockSpec(memory_space=pltpu.VMEM)] * 3,
        out_shape=[
            jax.ShapeDtypeStruct((PATCHES, PACKED, BINS), jnp.float32),
            jax.ShapeDtypeStruct((1, BINS), jnp.int32),
            jax.ShapeDtypeStruct((1, BINS), jnp.float32),
        ],
        name="pack",
    )(*smalls)


def send_flux(table, psf, image, packed, weight):
    return pl.pallas_call(
        flux_body,
        grid=(STEPS,),
        in_specs=[SMEM] * 2 + window_specs() + [whole(packed.shape), WEIGHT_BLOCK],
        out_specs=SEND_BLOCK,
        out_shape=jax.ShapeDtypeStruct(SEND_SHAPE, jnp.bfloat16),
        scratch_shapes=[
            GOOD_SCRATCH,
            BAND_SCRATCH,
            pltpu.VMEM((2 * GRID_ROWS, BINS), jnp.bfloat16),
        ],
        compiler_params=params(60),
        name="send_flux",
    )(table, psf, image, image, image, packed, weight)


def exchange(pieces, axes):
    return lax.all_to_all(pieces, axes, split_axis=0, concat_axis=0, tiled=True)


def strip(table, rows, received):
    return pl.pallas_call(
        strip_body,
        in_specs=[SMEM, SMEM, pl.BlockSpec(memory_space=pltpu.VMEM)],
        out_specs=pl.BlockSpec(memory_space=pltpu.VMEM),
        out_shape=jax.ShapeDtypeStruct((PATCHES, FRAME, LANES), jnp.bfloat16),
        scratch_shapes=[pltpu.VMEM((STRIP, LANES), jnp.float32)] * BANDS,
        compiler_params=pltpu.CompilerParams(vmem_limit_bytes=24 << 20),
        name="strip",
    )(table, rows, received.reshape(-1, PIECE_ROWS, LANES))


def spread(received):
    rows = FRAME // 3
    return pl.pallas_call(
        spread_body,
        grid=(3,),
        in_specs=[pl.BlockSpec((PATCHES, rows, LANES), lambda i: (0, i, 0))],
        out_specs=pl.BlockSpec((BANDS, rows, SPAN), lambda i: (0, i, 0)),
        out_shape=jax.ShapeDtypeStruct((BANDS, FRAME, SPAN), jnp.float32),
        compiler_params=params(24),
        name="spread",
    )(received)


def strip_rows(first):
    first = first.reshape(1, GROUPS * PIECES)
    blocks = [first]
    for k in range(1, VISITS):
        blocks.append(lax.ppermute(first, "visit", [(i, (i + k) % VISITS) for i in range(VISITS)]))
    return jnp.concatenate(blocks, axis=1).astype(jnp.int32).reshape(-1)


def shards(
    image,
    inv_var,
    bg_grid,
    bg_mix,
    psf_taps,
    warp_shift,
    bad_cols,
    piece_patch,
    piece_pos,
    band_of_visit,
):
    packed, table, psf = pack(
        bg_mix,
        piece_patch[0, :, 0],
        piece_pos,
        psf_taps,
        warp_shift,
        bad_cols,
        band_of_visit,
        bg_grid,
    )
    packed = lax.all_to_all(packed, "fp", split_axis=0, concat_axis=0, tiled=True)
    weight_pieces, weight = send_weight(table, psf, inv_var)
    both = ("visit", "fp")
    weight_arrived = exchange(weight_pieces, both)
    flux_pieces = send_flux(table, psf, image, packed, weight)
    rows = strip_rows(packed[:, GRID_ROWS, :PIECES])
    flux_pieces, rows = lax.optimization_barrier((flux_pieces, rows))
    flux_arrived = exchange(flux_pieces, both)
    weight_frames = exchange(strip(table, rows, weight_arrived), "fp")
    flux_frames = exchange(strip(table, rows, flux_arrived), "fp")
    return (spread(flux_frames)[:, None], spread(weight_frames)[:, None])


def solution(mesh):
    placed = (
        P("visit", "fp", None),
        P("visit", "fp", None),
        P("visit", "fp", None, None),
        P(),
        P("visit", "fp", None),
        P("visit", "fp"),
        P("fp", None),
        P("visit", "fp", None),
        P("visit", "fp"),
        P(),
    )
    return jax.shard_map(
        shards,
        mesh=mesh,
        in_specs=placed,
        out_specs=(P(None, "fp", None, "visit"), P(None, "fp", None, "visit")),
        check_vma=False,
    )
```

```python
import jax
import jax.numpy as jnp
from jax import lax
from jax.experimental import pallas as pl
from jax.experimental.pallas import tpu as pltpu
from jax.sharding import PartitionSpec as P

ROW_PIX = 4096
BANDS = 4
CCD_ROWS = 256
TAPS_HALF = 10
FRAME = 456
HALF = 16
PIECES = 16
PIECE_ROWS = 16
BINS = 128
BIN_PIX = ROW_PIX // BINS
PATCHES = 16
VISITS = 8
TURNS = VISITS // BANDS
GROUPS = 16
GRID_ROWS = 16
PACKED = GRID_ROWS + 8
BAD_COUNT = 32
AT_BAD = 16
AT_SHIFT = 48
AT_VISIT = 49
AT_ORDER = 56
SPAN = ROW_PIX // VISITS
PER = 4
PARTS = 4
THIRDS = 3
LANES = 128
SHARE = LANES // PARTS
PART_ROWS = CCD_ROWS // PARTS
STRIP = 16 * 256 + 208
STRIDE = 256
BLOCK = 256
PAD = 128
WINDOW = BLOCK + 2 * PAD
STEPS = VISITS // PER
WIDTH = SPAN * PER


def fill_band(table_ref, psf_ref, band_ref, absolute):
    shape = (16, WINDOW)
    step = lax.broadcasted_iota(jnp.int32, shape, 0) - 2
    lag = 3 * PAD - lax.broadcasted_iota(jnp.int32, shape, 1) - step
    offset = (table_ref[0, AT_SHIFT] - 16 * step).astype(jnp.float32) / 16.0
    angle = offset * jnp.float32(jnp.pi)
    safe = jnp.where(offset == 0.0, 1.0, angle)
    lanczos = jnp.where(
        offset == 0.0, 1.0, 3.0 * jnp.sin(safe) * jnp.sin(safe / 3.0) / (safe * safe)
    )
    lanczos = jnp.where((jnp.abs(offset) < 3.0) & (step < 7), lanczos, 0.0)
    lanczos = lanczos / jnp.sum(lanczos, axis=0, keepdims=True)
    taps = jnp.zeros(shape, jnp.float32)
    total = psf_ref[0, 0]
    for e in range(2 * TAPS_HALF + 1):
        value = psf_ref[0, e]
        taps = jnp.where(lag == e - TAPS_HALF, value, taps)
        total = total + value if e else total
    combined = jnp.sum(lanczos * (taps / total), axis=0, keepdims=True)
    combined = jnp.abs(combined) if absolute else combined
    rolled = pltpu.roll(
        jnp.broadcast_to(combined, (128, WINDOW)), 0, axis=1, stride=1, stride_axis=0
    ).astype(jnp.bfloat16)
    for i in range(WINDOW // 128):
        for o in range(BLOCK // 128):
            tile = (o - i) % (WINDOW // 128)
            band_ref[128 * i : 128 * (i + 1), 128 * o : 128 * (o + 1)] = rolled[
                :, 128 * tile : 128 * (tile + 1)
            ]


def fill_good(table_ref, good_ref):
    columns = lax.broadcasted_iota(jnp.int32, good_ref.shape, 1) - PAD
    good = (columns >= 0) & (columns < ROW_PIX)
    for k in range(BAD_COUNT):
        good = good & (columns != table_ref[0, AT_BAD + k])
    good_ref[...] = good.astype(jnp.float32)


def convolve(window, band_ref, span):
    parts = [
        jnp.dot(
            window[:, start : start + WINDOW], band_ref[...], preferred_element_type=jnp.float32
        )
        for start in range(span * SPAN, (span + 1) * SPAN, BLOCK)
    ]
    return jnp.concatenate(parts, axis=1)


def lane_part(shape):
    return lax.broadcasted_iota(jnp.int32, shape, 1) // SHARE


def swap_parts(blocks):
    part = lane_part(blocks[0].shape)
    even = part % 2 == 0
    low = part < 2

    def cross(a, b, mask, shift):
        first = jnp.where(mask, a, pltpu.roll(b, shift, axis=1))
        return first, jnp.where(mask, pltpu.roll(a, LANES - shift, axis=1), b)

    y0, y1 = cross(blocks[0], blocks[1], even, SHARE)
    y2, y3 = cross(blocks[2], blocks[3], even, SHARE)
    z0, z2 = cross(y0, y2, low, 2 * SHARE)
    z1, z3 = cross(y1, y3, low, 2 * SHARE)
    return z0, z1, z2, z3


def send_pieces(out_ref, span, values):
    for tile in range(SPAN // LANES):
        column = values[:, LANES * tile : LANES * (tile + 1)]
        blocks = [column[PART_ROWS * g : PART_ROWS * (g + 1)] for g in range(PARTS)]
        for k, block in enumerate(swap_parts(blocks)):
            out_ref[span * (SPAN // SHARE) + PARTS * tile + k] = block.astype(jnp.bfloat16)


def pack_body(
    mix_ref, patch_ref, pos_ref, psf_ref, shift_ref, bad_ref, band_ref, grid_ref, out_ref, table_ref, taps_ref
):
    group = lax.axis_index("fp")
    lane = lax.broadcasted_iota(jnp.int32, (1, BINS), 1)
    table = jnp.zeros((1, BINS), jnp.int32)
    first = table
    for j in range(PIECES):
        first = jnp.where(lane == j, patch_ref[j] * STRIDE + pos_ref[0, j], first)
    first = first.astype(jnp.float32)
    for q in range(PATCHES):
        out_ref[q, :GRID_ROWS] = grid_ref[0, 0] * mix_ref[q, group]
        out_ref[q, GRID_ROWS:] = jnp.broadcast_to(first, (PACKED - GRID_ROWS, BINS))
    for k in range(BAD_COUNT):
        table = jnp.where(lane == AT_BAD + k, bad_ref[0, k], table)
    table = jnp.where(lane == AT_SHIFT, shift_ref[0, 0], table)
    table = jnp.where(lane == AT_VISIT, lax.axis_index("visit"), table)
    bands = [band_ref[v] for v in range(VISITS)]
    for v in range(VISITS):
        place = bands[v] * TURNS
        for u in range(v):
            place = place + (bands[u] == bands[v]).astype(jnp.int32)
        table = jnp.where(lane == AT_ORDER + place, v, table)
    table_ref[...] = table
    taps = jnp.zeros((1, BINS), jnp.float32)
    for e in range(2 * TAPS_HALF + 1):
        taps = jnp.where(lane == e, psf_ref[0, 0, e], taps)
    taps_ref[...] = taps


def masked_window(good_ref, left_ref, mid_ref, right_ref):
    start = pl.multiple_of(pl.program_id(0) * WIDTH, 128)
    good = good_ref[:, pl.ds(start, WIDTH + 2 * PAD)]
    window = jnp.concatenate([left_ref[0], mid_ref[0], right_ref[0]], axis=1)
    return start, good, window * good.astype(jnp.bfloat16)


def weight_body(
    table_ref,
    psf_ref,
    left_ref,
    mid_ref,
    right_ref,
    send_ref,
    weight_ref,
    good_ref,
    band_ref,
):
    @pl.when(pl.program_id(0) == 0)
    def _():
        fill_good(table_ref, good_ref)
        fill_band(table_ref, psf_ref, band_ref, True)

    _, _, window = masked_window(good_ref, left_ref, mid_ref, right_ref)
    for span in range(PER):
        weight = convolve(window, band_ref, span)
        weight_ref[span] = weight.astype(jnp.bfloat16)
        send_pieces(send_ref, span, weight)


def flux_body(
    table_ref,
    psf_ref,
    left_ref,
    mid_ref,
    right_ref,
    packed_ref,
    weight_ref,
    send_ref,
    good_ref,
    band_ref,
    model_ref,
):
    @pl.when(pl.program_id(0) == 0)
    def _():
        fill_good(table_ref, good_ref)
        fill_band(table_ref, psf_ref, band_ref, False)
        model = packed_ref[0, :GRID_ROWS]
        for k in range(1, GROUPS):
            model = model + packed_ref[k, :GRID_ROWS]
        upper = model.astype(jnp.bfloat16)
        model_ref[:GRID_ROWS] = upper
        model_ref[GRID_ROWS:] = (model - upper.astype(jnp.float32)).astype(jnp.bfloat16)

    start, good, window = masked_window(good_ref, left_ref, mid_ref, right_ref)
    shape = (BINS, WIDTH + 2 * PAD)
    first = lax.broadcasted_iota(jnp.int32, shape, 0) * BIN_PIX
    column = lax.broadcasted_iota(jnp.int32, shape, 1) + (start - PAD)
    spread = ((column >= first) & (column < first + BIN_PIX)).astype(jnp.bfloat16)
    expanded = jnp.dot(model_ref[...], spread, preferred_element_type=jnp.float32) * good
    window = jnp.concatenate([window, expanded.astype(jnp.bfloat16)], axis=0)
    for span in range(PER):
        warped = convolve(window, band_ref, span)
        backdrop = warped[CCD_ROWS : CCD_ROWS + GRID_ROWS] + warped[CCD_ROWS + GRID_ROWS :]
        backdrop = jnp.broadcast_to(
            backdrop[:, None, :], (GRID_ROWS, CCD_ROWS // GRID_ROWS, SPAN)
        ).reshape(CCD_ROWS, SPAN)
        flux = warped[:CCD_ROWS] - backdrop
        send_pieces(send_ref, span, flux * weight_ref[span].astype(jnp.float32))


def strip_body(table_ref, rows_ref, received_ref, out_ref, *strips):
    for strip_ref in strips:
        strip_ref[...] = jnp.zeros(strip_ref.shape, strip_ref.dtype)
    part = lane_part((PIECE_ROWS, LANES))
    masks = [part == m for m in range(PARTS)]
    blocks = PART_ROWS // PIECE_ROWS

    def step(index, carry):
        turn = index // (GROUPS * blocks)
        group = index // blocks % GROUPS
        block = index % blocks
        work = []
        for band, strip_ref in enumerate(strips):
            visit = table_ref[0, AT_ORDER + TURNS * band + turn]
            value = received_ref[(visit * GROUPS + group) * blocks + block].astype(jnp.float32)
            own = table_ref[0, AT_VISIT]
            place = (((own >> 1) - (visit >> 1)) & (VISITS // 2 - 1)) * 2 + ((own ^ visit) & 1)
            base = (place * GROUPS + group) * PIECES
            for m in range(PARTS):
                row = rows_ref[base + blocks * m + block]
                work.append((strip_ref.at[pl.ds(row, PIECE_ROWS), :], value, masks[m]))
        sums = [ref[...] + value for ref, value, _ in work]
        for (ref, _, mask), total in zip(work, sums):
            pltpu.store(ref, total, mask=mask)
        return carry

    lax.fori_loop(0, TURNS * GROUPS * blocks, step, 0)
    part = lane_part((FRAME, LANES))
    even = part % 2 == 0
    low = part < 2

    def fold(a, b, mask, shift):
        return jnp.where(mask, a, b) + pltpu.roll(jnp.where(mask, b, a), shift, axis=1)

    for patch in range(PATCHES):
        frames = [strip_ref[STRIDE * patch : STRIDE * patch + FRAME] for strip_ref in strips]
        first = fold(frames[0], frames[1], even, SHARE)
        second = fold(frames[2], frames[3], even, SHARE)
        out_ref[patch] = fold(first, second, low, 2 * SHARE).astype(jnp.bfloat16)


def spread_body(received_ref, out_ref, taken_ref, given_ref, in_sems, out_sems):
    rows = FRAME // THIRDS
    reads = [
        pltpu.make_async_copy(
            received_ref.at[:, pl.ds(rows * n, rows)], taken_ref.at[n], in_sems.at[n]
        )
        for n in range(THIRDS)
    ]
    writes = [
        pltpu.make_async_copy(
            given_ref.at[n], out_ref.at[:, pl.ds(rows * n, rows)], out_sems.at[n]
        )
        for n in range(THIRDS)
    ]
    for read in reads:
        read.start()
    for n in range(THIRDS):
        reads[n].wait()
        for tile in range(SPAN // LANES):
            blocks = [taken_ref[n, PARTS * tile + m].astype(jnp.float32) for m in range(PARTS)]
            for band, block in enumerate(swap_parts(blocks)):
                given_ref[n, band, :, LANES * tile : LANES * (tile + 1)] = block
        writes[n].start()
    for write in writes:
        write.wait()


SMEM = pl.BlockSpec(memory_space=pltpu.SMEM)


def whole(shape):
    zeros = (0,) * len(shape)
    return pl.BlockSpec(shape, lambda i, *_: zeros)


def params(mebibytes):
    return pltpu.CompilerParams(
        dimension_semantics=("arbitrary",), vmem_limit_bytes=mebibytes << 20
    )


def window_specs():
    tiles = WIDTH // 128
    last = ROW_PIX // 128 - 1
    left = pl.BlockSpec((1, CCD_ROWS, 128), lambda i: (0, 0, jnp.maximum(i * tiles - 1, 0)))
    mid = pl.BlockSpec((1, CCD_ROWS, WIDTH), lambda i: (0, 0, i))
    right = pl.BlockSpec((1, CCD_ROWS, 128), lambda i: (0, 0, jnp.minimum((i + 1) * tiles, last)))
    return [left, mid, right]


SEND_SHAPE = (VISITS * GROUPS, PART_ROWS, LANES)
SEND_BLOCK = pl.BlockSpec((PER * GROUPS,) + SEND_SHAPE[1:], lambda i: (i, 0, 0))
WEIGHT_BLOCK = pl.BlockSpec((PER, CCD_ROWS, SPAN), lambda i: (i, 0, 0))
GOOD_SCRATCH = pltpu.VMEM((1, ROW_PIX + 2 * PAD), jnp.float32)
BAND_SCRATCH = pltpu.VMEM((WINDOW, BLOCK), jnp.bfloat16)


def send_weight(table, psf, inv_var):
    return pl.pallas_call(
        weight_body,
        grid=(STEPS,),
        in_specs=[SMEM] * 2 + window_specs(),
        out_specs=[SEND_BLOCK, WEIGHT_BLOCK],
        out_shape=[
            jax.ShapeDtypeStruct(SEND_SHAPE, jnp.bfloat16),
            jax.ShapeDtypeStruct((VISITS, CCD_ROWS, SPAN), jnp.bfloat16),
        ],
        scratch_shapes=[GOOD_SCRATCH, BAND_SCRATCH],
        compiler_params=params(60),
        name="send_weight",
    )(table, psf, inv_var, inv_var, inv_var)


def pack(*smalls):
    return pl.pallas_call(
        pack_body,
        in_specs=[SMEM] * (len(smalls) - 1) + [pl.BlockSpec(memory_space=pltpu.VMEM)],
        out_specs=[pl.BlockSpec(memory_space=pltpu.VMEM)] * 3,
        out_shape=[
            jax.ShapeDtypeStruct((PATCHES, PACKED, BINS), jnp.float32),
            jax.ShapeDtypeStruct((1, BINS), jnp.int32),
            jax.ShapeDtypeStruct((1, BINS), jnp.float32),
        ],
        name="pack",
    )(*smalls)


def send_flux(table, psf, image, packed, weight):
    return pl.pallas_call(
        flux_body,
        grid=(STEPS,),
        in_specs=[SMEM] * 2 + window_specs() + [whole(packed.shape), WEIGHT_BLOCK],
        out_specs=SEND_BLOCK,
        out_shape=jax.ShapeDtypeStruct(SEND_SHAPE, jnp.bfloat16),
        scratch_shapes=[
            GOOD_SCRATCH,
            BAND_SCRATCH,
            pltpu.VMEM((2 * GRID_ROWS, BINS), jnp.bfloat16),
        ],
        compiler_params=params(60),
        name="send_flux",
    )(table, psf, image, image, image, packed, weight)


def exchange(pieces, axes):
    return lax.all_to_all(pieces, axes, split_axis=0, concat_axis=0, tiled=True)


def strip(table, rows, received):
    return pl.pallas_call(
        strip_body,
        in_specs=[SMEM, SMEM, pl.BlockSpec(memory_space=pltpu.VMEM)],
        out_specs=pl.BlockSpec(memory_space=pltpu.VMEM),
        out_shape=jax.ShapeDtypeStruct((PATCHES, FRAME, LANES), jnp.bfloat16),
        scratch_shapes=[pltpu.VMEM((STRIP, LANES), jnp.float32)] * BANDS,
        compiler_params=pltpu.CompilerParams(vmem_limit_bytes=24 << 20),
        name="strip",
    )(table, rows, received.reshape(-1, PIECE_ROWS, LANES))


def spread(received):
    rows = FRAME // THIRDS
    anywhere = pl.BlockSpec(memory_space=pl.ANY)
    return pl.pallas_call(
        spread_body,
        in_specs=[anywhere],
        out_specs=anywhere,
        out_shape=jax.ShapeDtypeStruct((BANDS, FRAME, SPAN), jnp.float32),
        scratch_shapes=[
            pltpu.VMEM((THIRDS, PATCHES, rows, LANES), jnp.bfloat16),
            pltpu.VMEM((THIRDS, BANDS, rows, SPAN), jnp.float32),
            pltpu.SemaphoreType.DMA((THIRDS,)),
            pltpu.SemaphoreType.DMA((THIRDS,)),
        ],
        compiler_params=pltpu.CompilerParams(vmem_limit_bytes=24 << 20),
        name="spread",
    )(received)


def strip_rows(first):
    first = first.reshape(1, GROUPS * PIECES)
    other = lax.ppermute(first, "visit", [(i, i ^ 1) for i in range(VISITS)])
    pair = jnp.concatenate([first, other], axis=1)
    blocks = [pair]
    for k in range(2, VISITS, 2):
        blocks.append(lax.ppermute(pair, "visit", [(i, (i + k) % VISITS) for i in range(VISITS)]))
    return jnp.concatenate(blocks, axis=1).astype(jnp.int32).reshape(-1)


def shards(
    image,
    inv_var,
    bg_grid,
    bg_mix,
    psf_taps,
    warp_shift,
    bad_cols,
    piece_patch,
    piece_pos,
    band_of_visit,
):
    packed, table, psf = pack(
        bg_mix,
        piece_patch[0, :, 0],
        piece_pos,
        psf_taps,
        warp_shift,
        bad_cols,
        band_of_visit,
        bg_grid,
    )
    packed = lax.all_to_all(packed, "fp", split_axis=0, concat_axis=0, tiled=True)
    weight_pieces, weight = send_weight(table, psf, inv_var)
    both = ("visit", "fp")
    weight_arrived = exchange(weight_pieces, both)
    flux_pieces = send_flux(table, psf, image, packed, weight)
    rows = strip_rows(packed[:, GRID_ROWS, :PIECES])
    flux_pieces, rows = lax.optimization_barrier((flux_pieces, rows))
    flux_arrived = exchange(flux_pieces, both)
    weight_frames = exchange(strip(table, rows, weight_arrived), "fp")
    flux_frames = exchange(strip(table, rows, flux_arrived), "fp")
    return (spread(flux_frames)[:, None], spread(weight_frames)[:, None])


def solution(mesh):
    placed = (
        P("visit", "fp", None),
        P("visit", "fp", None),
        P("visit", "fp", None, None),
        P(),
        P("visit", "fp", None),
        P("visit", "fp"),
        P("fp", None),
        P("visit", "fp", None),
        P("visit", "fp"),
        P(),
    )
    return jax.shard_map(
        shards,
        mesh=mesh,
        in_specs=placed,
        out_specs=(P(None, "fp", None, "visit"), P(None, "fp", None, "visit")),
        check_vma=False,
    )
```

```python
import jax
import jax.numpy as jnp
from jax import lax
from jax.experimental import pallas as pl
from jax.experimental.pallas import tpu as pltpu
from jax.sharding import PartitionSpec as P

ROW_PIX = 4096
BANDS = 4
CCD_ROWS = 256
TAPS_HALF = 10
FRAME = 456
HALF = 16
PIECES = 16
PIECE_ROWS = 16
BINS = 128
BIN_PIX = ROW_PIX // BINS
PATCHES = 16
VISITS = 8
TURNS = VISITS // BANDS
GROUPS = 16
GRID_ROWS = 16
PACKED = GRID_ROWS + 8
BAD_COUNT = 32
AT_BAD = 16
AT_SHIFT = 48
AT_VISIT = 49
AT_ORDER = 56
SPAN = ROW_PIX // VISITS
PER = 4
PARTS = 4
THIRDS = 3
LANES = 128
SHARE = LANES // PARTS
PART_ROWS = CCD_ROWS // PARTS
STRIP = 16 * 256 + 208
STRIDE = 256
BLOCK = 256
PAD = 128
WINDOW = BLOCK + 2 * PAD
STEPS = VISITS // PER
WIDTH = SPAN * PER


def fill_band(table_ref, psf_ref, band_ref, absolute):
    shape = (16, WINDOW)
    step = lax.broadcasted_iota(jnp.int32, shape, 0) - 2
    lag = 3 * PAD - lax.broadcasted_iota(jnp.int32, shape, 1) - step
    offset = (table_ref[0, AT_SHIFT] - 16 * step).astype(jnp.float32) / 16.0
    angle = offset * jnp.float32(jnp.pi)
    safe = jnp.where(offset == 0.0, 1.0, angle)
    lanczos = jnp.where(
        offset == 0.0, 1.0, 3.0 * jnp.sin(safe) * jnp.sin(safe / 3.0) / (safe * safe)
    )
    lanczos = jnp.where((jnp.abs(offset) < 3.0) & (step < 7), lanczos, 0.0)
    lanczos = lanczos / jnp.sum(lanczos, axis=0, keepdims=True)
    taps = jnp.zeros(shape, jnp.float32)
    total = psf_ref[0, 0]
    for e in range(2 * TAPS_HALF + 1):
        value = psf_ref[0, e]
        taps = jnp.where(lag == e - TAPS_HALF, value, taps)
        total = total + value if e else total
    combined = jnp.sum(lanczos * (taps / total), axis=0, keepdims=True)
    combined = jnp.abs(combined) if absolute else combined
    rolled = pltpu.roll(
        jnp.broadcast_to(combined, (128, WINDOW)), 0, axis=1, stride=1, stride_axis=0
    ).astype(jnp.bfloat16)
    for i in range(WINDOW // 128):
        for o in range(BLOCK // 128):
            tile = (o - i) % (WINDOW // 128)
            band_ref[128 * i : 128 * (i + 1), 128 * o : 128 * (o + 1)] = rolled[
                :, 128 * tile : 128 * (tile + 1)
            ]


def fill_good(table_ref, good_ref):
    columns = lax.broadcasted_iota(jnp.int32, good_ref.shape, 1) - PAD
    good = (columns >= 0) & (columns < ROW_PIX)
    for k in range(BAD_COUNT):
        good = good & (columns != table_ref[0, AT_BAD + k])
    good_ref[...] = good.astype(jnp.float32)


def convolve(window, band_ref, span):
    parts = [
        jnp.dot(
            window[:, start : start + WINDOW], band_ref[...], preferred_element_type=jnp.float32
        )
        for start in range(span * SPAN, (span + 1) * SPAN, BLOCK)
    ]
    return jnp.concatenate(parts, axis=1)


def lane_part(shape):
    return lax.broadcasted_iota(jnp.int32, shape, 1) // SHARE


def swap_parts(blocks):
    part = lane_part(blocks[0].shape)
    even = part % 2 == 0
    low = part < 2

    def cross(a, b, mask, shift):
        first = jnp.where(mask, a, pltpu.roll(b, shift, axis=1))
        return first, jnp.where(mask, pltpu.roll(a, LANES - shift, axis=1), b)

    y0, y1 = cross(blocks[0], blocks[1], even, SHARE)
    y2, y3 = cross(blocks[2], blocks[3], even, SHARE)
    z0, z2 = cross(y0, y2, low, 2 * SHARE)
    z1, z3 = cross(y1, y3, low, 2 * SHARE)
    return z0, z1, z2, z3


def send_pieces(out_ref, span, values):
    for tile in range(SPAN // LANES):
        column = values[:, LANES * tile : LANES * (tile + 1)]
        blocks = [column[PART_ROWS * g : PART_ROWS * (g + 1)] for g in range(PARTS)]
        for k, block in enumerate(swap_parts(blocks)):
            out_ref[span * (SPAN // SHARE) + PARTS * tile + k] = block.astype(jnp.bfloat16)


def pack_body(
    mix_ref, patch_ref, pos_ref, psf_ref, bad_ref, band_ref, shift_ref, grid_ref, out_ref, table_ref, taps_ref
):
    group = lax.axis_index("fp")
    lane = lax.broadcasted_iota(jnp.int32, (1, BINS), 1)
    table = jnp.zeros((1, BINS), jnp.int32)
    first = table
    for j in range(PIECES):
        first = jnp.where(lane == j, patch_ref[j] * STRIDE + pos_ref[0, j], first)
    first = first.astype(jnp.float32)
    for q in range(PATCHES):
        out_ref[q, :GRID_ROWS] = grid_ref[0, 0] * mix_ref[q, group]
        out_ref[q, GRID_ROWS:] = jnp.broadcast_to(first, (PACKED - GRID_ROWS, BINS))
    for k in range(BAD_COUNT):
        table = jnp.where(lane == AT_BAD + k, bad_ref[0, k], table)
    table = jnp.where(lane == AT_SHIFT, shift_ref[...], table)
    table = jnp.where(lane == AT_VISIT, lax.axis_index("visit"), table)
    bands = [band_ref[v] for v in range(VISITS)]
    for v in range(VISITS):
        place = bands[v] * TURNS
        for u in range(v):
            place = place + (bands[u] == bands[v]).astype(jnp.int32)
        table = jnp.where(lane == AT_ORDER + place, v, table)
    table_ref[...] = table
    taps = jnp.zeros((1, BINS), jnp.float32)
    for e in range(2 * TAPS_HALF + 1):
        taps = jnp.where(lane == e, psf_ref[0, 0, e], taps)
    taps_ref[...] = taps


def masked_window(good_ref, left_ref, mid_ref, right_ref):
    start = pl.multiple_of(pl.program_id(0) * WIDTH, 128)
    good = good_ref[:, pl.ds(start, WIDTH + 2 * PAD)]
    window = jnp.concatenate([left_ref[0], mid_ref[0], right_ref[0]], axis=1)
    return start, good, window * good.astype(jnp.bfloat16)


def weight_body(
    table_ref,
    psf_ref,
    left_ref,
    mid_ref,
    right_ref,
    send_ref,
    weight_ref,
    good_ref,
    band_ref,
):
    @pl.when(pl.program_id(0) == 0)
    def _():
        fill_good(table_ref, good_ref)
        fill_band(table_ref, psf_ref, band_ref, True)

    _, _, window = masked_window(good_ref, left_ref, mid_ref, right_ref)
    for span in range(PER):
        weight = convolve(window, band_ref, span)
        weight_ref[span] = weight.astype(jnp.bfloat16)
        send_pieces(send_ref, span, weight)


def flux_body(
    table_ref,
    psf_ref,
    left_ref,
    mid_ref,
    right_ref,
    packed_ref,
    weight_ref,
    send_ref,
    good_ref,
    band_ref,
    model_ref,
):
    @pl.when(pl.program_id(0) == 0)
    def _():
        fill_good(table_ref, good_ref)
        fill_band(table_ref, psf_ref, band_ref, False)
        model = packed_ref[0, :GRID_ROWS]
        for k in range(1, GROUPS):
            model = model + packed_ref[k, :GRID_ROWS]
        upper = model.astype(jnp.bfloat16)
        model_ref[:GRID_ROWS] = upper
        model_ref[GRID_ROWS:] = (model - upper.astype(jnp.float32)).astype(jnp.bfloat16)

    start, good, window = masked_window(good_ref, left_ref, mid_ref, right_ref)
    shape = (BINS, WIDTH + 2 * PAD)
    first = lax.broadcasted_iota(jnp.int32, shape, 0) * BIN_PIX
    column = lax.broadcasted_iota(jnp.int32, shape, 1) + (start - PAD)
    spread = ((column >= first) & (column < first + BIN_PIX)).astype(jnp.bfloat16)
    expanded = jnp.dot(model_ref[...], spread, preferred_element_type=jnp.float32) * good
    window = jnp.concatenate([window, expanded.astype(jnp.bfloat16)], axis=0)
    for span in range(PER):
        warped = convolve(window, band_ref, span)
        backdrop = warped[CCD_ROWS : CCD_ROWS + GRID_ROWS] + warped[CCD_ROWS + GRID_ROWS :]
        backdrop = jnp.broadcast_to(
            backdrop[:, None, :], (GRID_ROWS, CCD_ROWS // GRID_ROWS, SPAN)
        ).reshape(CCD_ROWS, SPAN)
        flux = warped[:CCD_ROWS] - backdrop
        send_pieces(send_ref, span, flux * weight_ref[span].astype(jnp.float32))


def strip_body(table_ref, rows_ref, received_ref, out_ref, *strips):
    for strip_ref in strips:
        strip_ref[...] = jnp.zeros(strip_ref.shape, strip_ref.dtype)
    part = lane_part((PIECE_ROWS, LANES))
    masks = [part == m for m in range(PARTS)]
    blocks = PART_ROWS // PIECE_ROWS

    def step(index, carry):
        turn = index // (GROUPS * blocks)
        group = index // blocks % GROUPS
        block = index % blocks
        work = []
        for band, strip_ref in enumerate(strips):
            visit = table_ref[0, AT_ORDER + TURNS * band + turn]
            value = received_ref[(visit * GROUPS + group) * blocks + block].astype(jnp.float32)
            own = table_ref[0, AT_VISIT]
            place = (((own >> 1) - (visit >> 1)) & (VISITS // 2 - 1)) * 2 + ((own ^ visit) & 1)
            base = (place * GROUPS + group) * PIECES
            for m in range(PARTS):
                row = rows_ref[base + blocks * m + block]
                work.append((strip_ref.at[pl.ds(row, PIECE_ROWS), :], value, masks[m]))
        sums = [ref[...] + value for ref, value, _ in work]
        for (ref, _, mask), total in zip(work, sums):
            pltpu.store(ref, total, mask=mask)
        return carry

    lax.fori_loop(0, TURNS * GROUPS * blocks, step, 0)
    part = lane_part((FRAME, LANES))
    even = part % 2 == 0
    low = part < 2

    def fold(a, b, mask, shift):
        return jnp.where(mask, a, b) + pltpu.roll(jnp.where(mask, b, a), shift, axis=1)

    for patch in range(PATCHES):
        frames = [strip_ref[STRIDE * patch : STRIDE * patch + FRAME] for strip_ref in strips]
        first = fold(frames[0], frames[1], even, SHARE)
        second = fold(frames[2], frames[3], even, SHARE)
        out_ref[patch] = fold(first, second, low, 2 * SHARE).astype(jnp.bfloat16)


def spread_body(received_ref, out_ref, taken_ref, given_ref, in_sem, out_sems):
    rows = FRAME // THIRDS
    read = pltpu.make_async_copy(received_ref, taken_ref, in_sem)
    writes = [
        pltpu.make_async_copy(
            given_ref.at[n], out_ref.at[:, pl.ds(rows * n, rows)], out_sems.at[n]
        )
        for n in range(THIRDS)
    ]
    read.start()
    shape = (PARTS * LANES, PARTS * LANES)
    lane = lax.broadcasted_iota(jnp.int32, shape, 0)
    column = lax.broadcasted_iota(jnp.int32, shape, 1)
    source = (column // SHARE % PARTS) * LANES + (column // LANES) * SHARE + column % SHARE
    order = (lane == source).astype(jnp.bfloat16)
    read.wait()
    for n in range(THIRDS):
        for tile in range(SPAN // LANES):
            blocks = [taken_ref[PARTS * tile + m, rows * n : rows * (n + 1)] for m in range(PARTS)]
            mixed = jnp.dot(
                jnp.concatenate(blocks, axis=1), order, preferred_element_type=jnp.float32
            )
            for band in range(BANDS):
                given_ref[n, band, :, LANES * tile : LANES * (tile + 1)] = mixed[
                    :, LANES * band : LANES * (band + 1)
                ]
        writes[n].start()
    for write in writes:
        write.wait()


SMEM = pl.BlockSpec(memory_space=pltpu.SMEM)


def whole(shape):
    zeros = (0,) * len(shape)
    return pl.BlockSpec(shape, lambda i, *_: zeros)


def params(mebibytes):
    return pltpu.CompilerParams(
        dimension_semantics=("arbitrary",), vmem_limit_bytes=mebibytes << 20
    )


def window_specs():
    tiles = WIDTH // 128
    last = ROW_PIX // 128 - 1
    left = pl.BlockSpec((1, CCD_ROWS, 128), lambda i: (0, 0, jnp.maximum(i * tiles - 1, 0)))
    mid = pl.BlockSpec((1, CCD_ROWS, WIDTH), lambda i: (0, 0, i))
    right = pl.BlockSpec((1, CCD_ROWS, 128), lambda i: (0, 0, jnp.minimum((i + 1) * tiles, last)))
    return [left, mid, right]


SEND_SHAPE = (VISITS * GROUPS, PART_ROWS, LANES)
SEND_BLOCK = pl.BlockSpec((PER * GROUPS,) + SEND_SHAPE[1:], lambda i: (i, 0, 0))
WEIGHT_BLOCK = pl.BlockSpec((PER, CCD_ROWS, SPAN), lambda i: (i, 0, 0))
GOOD_SCRATCH = pltpu.VMEM((1, ROW_PIX + 2 * PAD), jnp.float32)
BAND_SCRATCH = pltpu.VMEM((WINDOW, BLOCK), jnp.bfloat16)


def send_weight(table, psf, inv_var):
    return pl.pallas_call(
        weight_body,
        grid=(STEPS,),
        in_specs=[SMEM] * 2 + window_specs(),
        out_specs=[SEND_BLOCK, WEIGHT_BLOCK],
        out_shape=[
            jax.ShapeDtypeStruct(SEND_SHAPE, jnp.bfloat16),
            jax.ShapeDtypeStruct((VISITS, CCD_ROWS, SPAN), jnp.bfloat16),
        ],
        scratch_shapes=[GOOD_SCRATCH, BAND_SCRATCH],
        compiler_params=params(60),
        name="send_weight",
    )(table, psf, inv_var, inv_var, inv_var)


def pack(*smalls):
    return pl.pallas_call(
        pack_body,
        in_specs=[SMEM] * (len(smalls) - 2) + [pl.BlockSpec(memory_space=pltpu.VMEM)] * 2,
        out_specs=[pl.BlockSpec(memory_space=pltpu.VMEM)] * 3,
        out_shape=[
            jax.ShapeDtypeStruct((PATCHES, PACKED, BINS), jnp.float32),
            jax.ShapeDtypeStruct((1, BINS), jnp.int32),
            jax.ShapeDtypeStruct((1, BINS), jnp.float32),
        ],
        name="pack",
    )(*smalls)


def send_flux(table, psf, image, packed, weight):
    return pl.pallas_call(
        flux_body,
        grid=(STEPS,),
        in_specs=[SMEM] * 2 + window_specs() + [whole(packed.shape), WEIGHT_BLOCK],
        out_specs=SEND_BLOCK,
        out_shape=jax.ShapeDtypeStruct(SEND_SHAPE, jnp.bfloat16),
        scratch_shapes=[
            GOOD_SCRATCH,
            BAND_SCRATCH,
            pltpu.VMEM((2 * GRID_ROWS, BINS), jnp.bfloat16),
        ],
        compiler_params=params(60),
        name="send_flux",
    )(table, psf, image, image, image, packed, weight)


def exchange(pieces, axes):
    return lax.all_to_all(pieces, axes, split_axis=0, concat_axis=0, tiled=True)


def strip(table, rows, received):
    return pl.pallas_call(
        strip_body,
        in_specs=[SMEM, SMEM, pl.BlockSpec(memory_space=pltpu.VMEM)],
        out_specs=pl.BlockSpec(memory_space=pltpu.VMEM),
        out_shape=jax.ShapeDtypeStruct((PATCHES, FRAME, LANES), jnp.bfloat16),
        scratch_shapes=[pltpu.VMEM((STRIP, LANES), jnp.float32)] * BANDS,
        compiler_params=pltpu.CompilerParams(vmem_limit_bytes=24 << 20),
        name="strip",
    )(table, rows, received.reshape(-1, PIECE_ROWS, LANES))


def spread(received):
    rows = FRAME // THIRDS
    anywhere = pl.BlockSpec(memory_space=pl.ANY)
    return pl.pallas_call(
        spread_body,
        in_specs=[anywhere],
        out_specs=anywhere,
        out_shape=jax.ShapeDtypeStruct((BANDS, FRAME, SPAN), jnp.float32),
        scratch_shapes=[
            pltpu.VMEM((PATCHES, FRAME, LANES), jnp.bfloat16),
            pltpu.VMEM((THIRDS, BANDS, rows, SPAN), jnp.float32),
            pltpu.SemaphoreType.DMA,
            pltpu.SemaphoreType.DMA((THIRDS,)),
        ],
        compiler_params=pltpu.CompilerParams(vmem_limit_bytes=24 << 20),
        name="spread",
    )(received)


def strip_rows(first):
    first = first.reshape(1, GROUPS * PIECES)
    other = lax.ppermute(first, "visit", [(i, i ^ 1) for i in range(VISITS)])
    pair = jnp.concatenate([first, other], axis=1)
    blocks = [pair]
    for k in range(2, VISITS, 2):
        blocks.append(lax.ppermute(pair, "visit", [(i, (i + k) % VISITS) for i in range(VISITS)]))
    return jnp.concatenate(blocks, axis=1).astype(jnp.int32).reshape(-1)


def shards(
    image,
    inv_var,
    bg_grid,
    bg_mix,
    psf_taps,
    warp_shift,
    bad_cols,
    piece_patch,
    piece_pos,
    band_of_visit,
):
    packed, table, psf = pack(
        bg_mix,
        piece_patch[0, :, 0],
        piece_pos,
        psf_taps,
        bad_cols,
        band_of_visit,
        warp_shift,
        bg_grid,
    )
    packed = lax.all_to_all(packed, "fp", split_axis=0, concat_axis=0, tiled=True)
    weight_pieces, weight = send_weight(table, psf, inv_var)
    both = ("visit", "fp")
    weight_arrived = exchange(weight_pieces, both)
    flux_pieces = send_flux(table, psf, image, packed, weight)
    rows = strip_rows(packed[:, GRID_ROWS, :PIECES])
    flux_pieces, rows = lax.optimization_barrier((flux_pieces, rows))
    flux_arrived = exchange(flux_pieces, both)
    weight_frames = exchange(strip(table, rows, weight_arrived), "fp")
    flux_frames = exchange(strip(table, rows, flux_arrived), "fp")
    return (spread(flux_frames)[:, None], spread(weight_frames)[:, None])


def solution(mesh):
    placed = (
        P("visit", "fp", None),
        P("visit", "fp", None),
        P("visit", "fp", None, None),
        P(),
        P("visit", "fp", None),
        P("visit", "fp"),
        P("fp", None),
        P("visit", "fp", None),
        P("visit", "fp"),
        P(),
    )
    return jax.shard_map(
        shards,
        mesh=mesh,
        in_specs=placed,
        out_specs=(P(None, "fp", None, "visit"), P(None, "fp", None, "visit")),
        check_vma=False,
    )
```
